128 devices in a mesh: blk: 8 (over z, y_hi), grp: 16 (over y_lo, x, core).
Axes of the slice: x: 4, y: 4 (y_hi: 2, y_lo: 2; y = y_hi * 2 + y_lo), z: 4, core: 2. Of those that a mesh axis runs over, the one named last changes fastest.
Arguments:
- obj_query: bfloat16 [8192, 1536], P(('blk', 'grp')), may hold values from -64 to 64
- grad_out: bfloat16 [8192, 1536], P(('blk', 'grp')), may hold values from -256 to 256
- pattern_key: bfloat16 [8192, 1536], P('grp'), may hold values from -4.5 to 4.5
- pattern_value: bfloat16 [8192, 1536], P('grp'), may hold values from -6 to 6
- pencil_order: int32 [512], replicated, may hold values from 0 to 511, as said below
Outputs:
- query_grad: bfloat16 [8192, 1536], P(('blk', 'grp'))
- key_grad: bfloat16 [8192, 1536], P(('blk', 'grp'))
- value_grad: bfloat16 [8192, 1536], P(('blk', 'grp'))
The draws below stay inside these ranges and needn't reach their ends.
Inputs may be any that keep to these rules, and one draw needn't show every extreme that they name: pencil_order is a permutation of 0 to 511. With c the number of devices along grp, block r of the encoder's layout lies on the device of index r // 4 of the axes blk+grp, and pencil_order[r] names a block of pattern rows g * 512 to (g + 1) * 512 - 1, where g is that device index mod c.
All inputs are finite; a program needn't handle non-finite values.
Results may differ from the reference program's by a relative error of at most 0.0051.
Values may be sent and summed in bfloat16 or wider, within the bound.
No kernel may reach another device: no remote copies, remote signals or barrier semaphores. Data moves between devices by JAX's collectives and lax.ppermute only.
A program may use at most 128 MiB of HBM per device.

```python
import math
import jax
import jax.numpy as jnp
from jax import lax

D = 1536
H = 16
PD = 64
PENCIL = 16
NQ = 8192
NK = 8192
N_BLK = 8
N_GRP = 16


def base_keys(key):
    inner_key = jax.random.fold_in(key, 7)
    key_table = jnp.clip(jax.random.normal(inner_key, (NK, D), jnp.float32), -4.5, 4.5)
    return key_table.astype(jnp.bfloat16).astype(jnp.float32)


def draw_pattern_key(key, part):
    return base_keys(key).astype(jnp.bfloat16)


def draw_obj_query(key, part):
    inner_key = jax.random.fold_in(key, 11)
    query_table = jnp.clip(jax.random.normal(inner_key, (NQ, D), jnp.float32), -4.5, 4.5)
    return query_table.astype(jnp.bfloat16)


def draw_pencil_order(key, part):
    per_block = PD // PENCIL
    column_blocks = N_BLK * per_block

    def column_order(column):
        return jax.random.permutation(jax.random.fold_in(key, column), column_blocks)
    orders = jax.vmap(column_order)(jnp.arange(N_GRP, dtype=jnp.int32))
    blocks = jnp.arange(NK // PENCIL, dtype=jnp.int32)
    device = blocks // per_block
    column = device % N_GRP
    chosen = orders[column, device // N_GRP * per_block + blocks % per_block]
    return (column * column_blocks + chosen).astype(jnp.int32)


def level_of(own_key, dims, cuts, smallest, top_value):
    loudness, own = 1.0, jax.random.fold_in(own_key, 6)
    for position, blocks in cuts:
        steps = jnp.exp(jax.random.uniform(jax.random.fold_in(own, position), (blocks,), jnp.float32, smallest / len(cuts), top_value / len(cuts)))
        loudness = loudness * jnp.repeat(steps, dims[position] // blocks).reshape([-1 if axis == position else 1 for axis in range(len(dims))])
    return loudness


def gaussian(key, dims, deviation, limit, cuts=(), kind=jnp.bfloat16):
    entries = deviation * jax.random.normal(key, dims, jnp.float32)
    if cuts:
        entries = entries * level_of(key, dims, cuts, -0.22, 0.18)
    return jnp.clip(entries, -limit, limit).astype(kind)


def setup_inputs(seed: int = 0) -> dict:
    key_list = jax.random.split(jax.random.key(seed), 6)
    obj_query = draw_obj_query(jax.random.fold_in(key_list[5], 71), 0)
    grad_out = gaussian(key_list[1], (NQ, D), 48, 256.0, ((0, 128),))
    pattern_key = draw_pattern_key(jax.random.fold_in(key_list[5], 71), 0)
    pattern_value = gaussian(key_list[3], (NK, D), 1.0, 6.0, ((0, 16),))
    pencil_order = draw_pencil_order(jax.random.fold_in(key_list[5], 71), 0)
    return {"obj_query": obj_query, "grad_out": grad_out, "pattern_key": pattern_key, "pattern_value": pattern_value, "pencil_order": pencil_order}


def split_heads(matrix):
    return matrix.reshape(matrix.shape[0], H, matrix.shape[1] // H)

def reference(obj_query, grad_out, pattern_key, pattern_value, pencil_order):
    scaling = 1.0 / math.sqrt(D // H)
    key_heads = split_heads(pattern_key.astype(jnp.float32))
    value_heads = split_heads(pattern_value.astype(jnp.float32))
    blocking = math.gcd(NQ, 256)
    sweeps = NQ // blocking

    def sweep(carried, segment):
        keys_acc, values_acc = carried
        query_heads = split_heads(segment[0].astype(jnp.float32))
        grad_heads = split_heads(segment[1].astype(jnp.float32))
        scores = jnp.einsum('rhd,chd->hrc', query_heads, key_heads) * scaling
        prob_grad = jnp.einsum('rhd,chd->hrc', grad_heads, value_heads)
        highest = lax.optimization_barrier(jnp.max(scores, axis=2))
        weights = jnp.exp(scores - highest[:, :, None])
        totals = lax.optimization_barrier(jnp.sum(weights, axis=2))
        log_totals = highest + jnp.log(totals)
        mean_grads = lax.optimization_barrier(jnp.sum(weights * prob_grad, axis=2)) / totals
        softmax = jnp.exp(scores - log_totals[:, :, None])
        softmax_low = lax.optimization_barrier(softmax.astype(jnp.bfloat16)).astype(jnp.float32)
        score_grad = lax.optimization_barrier((scaling * softmax * (prob_grad - mean_grads[:, :, None])).astype(jnp.bfloat16)).astype(jnp.float32)
        query_term = jnp.einsum('hrc,chd->rhd', score_grad, key_heads).reshape(blocking, D)
        keys_acc = keys_acc + jnp.einsum('hrc,rhd->chd', score_grad, query_heads).reshape(NK, D)
        values_acc = values_acc + jnp.einsum('hrc,rhd->chd', softmax_low, grad_heads).reshape(NK, D)
        return ((keys_acc, values_acc), query_term.astype(jnp.bfloat16))
    zeros_acc = jnp.zeros((NK, D), jnp.float32)
    segments = (obj_query.reshape(sweeps, blocking, D), grad_out.reshape(sweeps, blocking, D))
    (keys_acc, values_acc), pieces = lax.scan(sweep, (zeros_acc, zeros_acc), segments)
    positions = jnp.arange(NK, dtype=jnp.int32)
    source = (pencil_order[positions // PENCIL] * PENCIL + positions % PENCIL).astype(jnp.int32)
    query_grad = pieces.reshape(NQ, D)
    key_grad = keys_acc[source].astype(jnp.bfloat16)
    value_grad = values_acc[source].astype(jnp.bfloat16)
    return (query_grad, key_grad, value_grad)
```

```python
import functools
import math

import jax
import jax.numpy as jnp
from jax import lax
from jax.experimental import pallas as pl
from jax.experimental.pallas import tpu as pltpu
from jax.sharding import Mesh
from jax.sharding import PartitionSpec as P

D = 1536
H = 16
HD = D // H
PENCIL = 16
PD = 64
HALF = PD // 2
WIDE = 4 * HD
N_Z = 4
N_Y = 2
N_G = 16
GRP = ("grp_0", "grp_1", "grp_2")
BLK_GRP = ("blk_0", "blk_1", "grp_0", "grp_1", "grp_2")
SCALE = 1.0 / math.sqrt(HD)
C2 = SCALE * math.log2(math.e)
TQ = 256
TK = 512
NEG = -1e30
F32 = jnp.float32
BF16 = jnp.bfloat16
CONTRACT_LAST = (((1,), (1,)), ((), ()))
CONTRACT_FIRST = (((0,), (0,)), ((), ()))


def mm(a, b, dims=(((1,), (0,)), ((), ()))):
    return lax.dot_general(a, b, dims, preferred_element_type=F32)


def pack_kernel(order_ref, place_ref, q_ref, g_ref, k_ref, v_ref, out_ref):
    y = place_ref[0]
    g = place_ref[1]
    for zt in range(N_Z):
        for part in range(PD // PENCIL):
            target = ((zt * N_Y + y) * N_G + g) * (PD // PENCIL) + part
            start = pl.multiple_of((order_ref[target] - g * (N_Z * N_Y * PD // PENCIL)) * PENCIL, PENCIL)
            keys = k_ref[pl.ds(start, PENCIL), :]
            values = v_ref[pl.ds(start, PENCIL), :]
            row = zt * HALF + part % 2 * PENCIL
            lane = part // 2 * 2 * HD
            for h in range(H):
                out_ref[h, row : row + PENCIL, lane : lane + HD] = keys[:, h * HD : (h + 1) * HD]
                out_ref[h, row : row + PENCIL, lane + HD : lane + 2 * HD] = values[:, h * HD : (h + 1) * HD]
    base = N_Z * HALF
    for half in range(2):
        lane = half * 2 * HD
        queries = q_ref[half * HALF : (half + 1) * HALF, :]
        grads = g_ref[half * HALF : (half + 1) * HALF, :]
        for h in range(H):
            out_ref[h, base : base + HALF, lane : lane + HD] = queries[:, h * HD : (h + 1) * HD]
            out_ref[h, base : base + HALF, lane + HD : lane + 2 * HD] = grads[:, h * HD : (h + 1) * HD]


def pack(order, place, obj_query, grad_out, pattern_key, pattern_value):
    vmem = pl.BlockSpec(memory_space=pltpu.VMEM)
    return pl.pallas_call(
        pack_kernel,
        out_shape=jax.ShapeDtypeStruct((H, N_Z * HALF + HALF, WIDE), BF16),
        in_specs=[pl.BlockSpec(memory_space=pltpu.SMEM), pl.BlockSpec(memory_space=pltpu.SMEM), vmem, vmem, vmem, vmem],
        out_specs=vmem,
        name="pack",
    )(order, place, obj_query, grad_out, pattern_key, pattern_value)


PK = N_G * N_Z * HALF
PQ = N_G * HALF


def unpack_keys(kv_ref, k_s, v_s):
    for half in range(2):
        for src in range(N_G):
            rows = slice(half * PK + src * N_Z * HALF, half * PK + (src + 1) * N_Z * HALF)
            lane = half * 2 * HD
            k_s[rows, :] = kv_ref[src, : N_Z * HALF, lane : lane + HD]
            v_s[rows, :] = kv_ref[src, : N_Z * HALF, lane + HD : lane + 2 * HD]


def unpack_queries(q_ref, q_s, g_s, base):
    for half in range(2):
        for src in range(N_G):
            rows = slice(base + half * PQ + src * HALF, base + half * PQ + (src + 1) * HALF)
            lane = half * 2 * HD
            q_s[rows, :] = q_ref[src, :, lane : lane + HD]
            g_s[rows, :] = q_ref[src, :, lane + HD : lane + 2 * HD]


def stats_kernel(q_ref, kv_ref, st_ref, q_s, g_s, k_s, v_s):
    unpack_keys(kv_ref, k_s, v_s)
    unpack_queries(q_ref, q_s, g_s, 0)

    def one_tile(t, _):
        q0 = pl.multiple_of(t * TQ, TQ)
        qt = q_s[pl.ds(q0, TQ), :]
        gt = g_s[pl.ds(q0, TQ), :]

        def one_chunk(j, carry):
            m, l, w = carry
            k0 = pl.multiple_of(j * TK, TK)
            s = mm(k_s[pl.ds(k0, TK), :], qt, CONTRACT_LAST).reshape(TK // 8, 8, TQ)
            d = mm(v_s[pl.ds(k0, TK), :], gt, CONTRACT_LAST).reshape(TK // 8, 8, TQ)
            top = jnp.maximum(m, jnp.max(s, axis=0))
            fade = jnp.exp2((m - top) * C2)
            e = jnp.exp2((s - top[None]) * C2)
            return top, l * fade + jnp.sum(e, axis=0), w * fade + jnp.sum(e * d, axis=0)

        zero = jnp.zeros((8, TQ), F32)
        m, l, w = lax.fori_loop(0, 2 * PK // TK, one_chunk, (jnp.full((8, TQ), NEG, F32), zero, zero), unroll=2)
        top = jnp.max(m, axis=0, keepdims=True)
        fade = jnp.exp2((m - top) * C2)
        st_ref[0:1, pl.ds(q0, TQ)] = top
        st_ref[1:2, pl.ds(q0, TQ)] = jnp.sum(l * fade, axis=0, keepdims=True)
        st_ref[2:3, pl.ds(q0, TQ)] = jnp.sum(w * fade, axis=0, keepdims=True)
        return 0

    lax.fori_loop(0, 2 * PQ // TQ, one_tile, 0)
    st_ref[3:8, :] = jnp.zeros((5, 2 * PQ), F32)


def stats(q, kv):
    vmem = pl.BlockSpec(memory_space=pltpu.VMEM)
    return pl.pallas_call(
        stats_kernel,
        out_shape=jax.ShapeDtypeStruct((8, 2 * PQ), F32),
        in_specs=[vmem, vmem],
        out_specs=vmem,
        scratch_shapes=[pltpu.VMEM((2 * PQ, HD), BF16)] * 2 + [pltpu.VMEM((2 * PK, HD), BF16)] * 2,
        name="stats",
    )(q, kv)


def joined(mine, theirs):
    top = jnp.maximum(mine[0:1], theirs[0:1])
    a = jnp.exp2((mine[0:1] - top) * C2)
    b = jnp.exp2((theirs[0:1] - top) * C2)
    total = mine[1:2] * a + theirs[1:2] * b
    return top * C2 + jnp.log2(total), (mine[2:3] * a + theirs[2:3] * b) / total


def grads_kernel(
    place_ref, qa_ref, qb_ref, kv_ref, sa_ref, sb_ref, ta_ref, tb_ref, dq_ref, dkv_ref,
    q_s, g_s, k_s, v_s, dq_s, dk_s, dv_s, log_s, mean_s,
):
    unpack_keys(kv_ref, k_s, v_s)
    unpack_queries(qa_ref, q_s, g_s, 0)
    unpack_queries(qb_ref, q_s, g_s, 2 * PQ)
    for n, (mine, theirs) in enumerate(((sa_ref, tb_ref), (sb_ref, ta_ref))):
        log_now, mean_now = joined(mine, theirs)
        log_s[:, n * 2 * PQ : (n + 1) * 2 * PQ] = jnp.broadcast_to(log_now, (8, 2 * PQ))
        mean_s[:, n * 2 * PQ : (n + 1) * 2 * PQ] = jnp.broadcast_to(mean_now, (8, 2 * PQ))
    dq_s[...] = jnp.zeros_like(dq_s)

    def one_chunk(j, _):
        k0 = pl.multiple_of(j * TK, TK)
        kc = k_s[pl.ds(k0, TK), :]
        vc = v_s[pl.ds(k0, TK), :]

        def one_tile(t, carry):
            dk, dv = carry
            q0 = pl.multiple_of(t * TQ, TQ)
            qt = q_s[pl.ds(q0, TQ), :]
            gt = g_s[pl.ds(q0, TQ), :]
            s = mm(kc, qt, CONTRACT_LAST).reshape(TK // 8, 8, TQ)
            d = mm(vc, gt, CONTRACT_LAST).reshape(TK // 8, 8, TQ)
            p = jnp.exp2(s * C2 - log_s[:, pl.ds(q0, TQ)][None])
            sg = ((d - mean_s[:, pl.ds(q0, TQ)][None]) * (p * SCALE)).astype(BF16).reshape(TK, TQ)
            p = p.astype(BF16).reshape(TK, TQ)
            dq_s[pl.ds(q0, TQ), :] += mm(sg, kc, CONTRACT_FIRST)
            return dk + mm(sg, qt), dv + mm(p, gt)

        zero = jnp.zeros((TK, HD), F32)
        dk, dv = lax.fori_loop(0, 4 * PQ // TQ, one_tile, (zero, zero), unroll=2)
        dk_s[pl.ds(k0, TK), :] = dk.astype(BF16)
        dv_s[pl.ds(k0, TK), :] = dv.astype(BF16)
        return 0

    lax.fori_loop(0, 2 * PK // TK, one_chunk, 0)
    for half in range(2):
        lane = half * 2 * HD
        for src in range(N_G):
            for zt in range(N_Z):
                r0 = half * PK + (src * N_Z + zt) * HALF
                dkv_ref[zt, src, :, lane : lane + HD] = dk_s[r0 : r0 + HALF, :]
                dkv_ref[zt, src, :, lane + HD : lane + 2 * HD] = dv_s[r0 : r0 + HALF, :]
    y = place_ref[0]
    for n, where in enumerate((y, 1 - y)):
        for src in range(N_G):
            for quarter in range(4):
                r0 = n * 2 * PQ + quarter // 2 * PQ + src * HALF + quarter % 2 * PENCIL
                dq_ref[where, src, :, quarter * HD : (quarter + 1) * HD] = dq_s[r0 : r0 + PENCIL, :].astype(BF16)


def grads(place, qa, qb, kv, sa, sb, ta, tb):
    vmem = pl.BlockSpec(memory_space=pltpu.VMEM)
    return pl.pallas_call(
        grads_kernel,
        out_shape=(
            jax.ShapeDtypeStruct((N_Y, N_G, PENCIL, WIDE), BF16),
            jax.ShapeDtypeStruct((N_Z, N_G, HALF, WIDE), BF16),
        ),
        in_specs=[pl.BlockSpec(memory_space=pltpu.SMEM)] + [vmem] * 7,
        out_specs=(vmem, vmem),
        scratch_shapes=[pltpu.VMEM((4 * PQ, HD), BF16)] * 2
        + [pltpu.VMEM((2 * PK, HD), BF16)] * 2
        + [pltpu.VMEM((4 * PQ, HD), F32)]
        + [pltpu.VMEM((2 * PK, HD), BF16)] * 2
        + [pltpu.VMEM((8, 4 * PQ), F32)] * 2,
        name="grads",
    )(place, qa, qb, kv, sa, sb, ta, tb)


def keys_out_kernel(got_ref, key_ref, value_ref):
    for h in range(H):
        total = got_ref[0, h].astype(F32)
        for z in range(1, N_Z):
            total = total + got_ref[z, h].astype(F32)
        total = total.astype(BF16)
        for half in range(2):
            lane = half * 2 * HD
            rows = slice(half * HALF, (half + 1) * HALF)
            key_ref[rows, h * HD : (h + 1) * HD] = total[:, lane : lane + HD]
            value_ref[rows, h * HD : (h + 1) * HD] = total[:, lane + HD : lane + 2 * HD]


def queries_out_kernel(got_ref, query_ref):
    for h in range(H):
        total = (got_ref[0, h].astype(F32) + got_ref[1, h].astype(F32)).astype(BF16)
        for quarter in range(4):
            rows = slice(quarter * PENCIL, (quarter + 1) * PENCIL)
            query_ref[rows, h * HD : (h + 1) * HD] = total[:, quarter * HD : (quarter + 1) * HD]


def placed_out(kernel, got, outs, name):
    vmem = pl.BlockSpec(memory_space=pltpu.VMEM)
    return pl.pallas_call(
        kernel,
        out_shape=[jax.ShapeDtypeStruct((PD, D), BF16)] * outs,
        in_specs=[vmem],
        out_specs=[vmem] * outs,
        name=name,
    )(got)


def on_device(obj_query, grad_out, pattern_key, pattern_value, pencil_order):
    place = jnp.stack([lax.axis_index("blk_1"), lax.axis_index(GRP)]).astype(jnp.int32)
    swap = functools.partial(lax.ppermute, axis_name="blk_1", perm=((0, 1), (1, 0)))
    sent = pack(pencil_order, place, obj_query, grad_out, pattern_key, pattern_value)
    got = lax.all_to_all(sent, GRP, 0, 0, tiled=True)
    qa = got[:, N_Z * HALF :, :]
    qb = swap(qa)
    sa = stats(qa, got)
    ta = swap(sa)
    sb = stats(qb, got)
    tb = swap(sb)
    dq, dkv = grads(place, qa, qb, got, sa, sb, ta, tb)
    dkv = lax.all_to_all(dkv.reshape(N_Z * N_G, HALF, WIDE), ("blk_0", *GRP), 0, 0, tiled=True)
    dq = lax.all_to_all(dq.reshape(N_Y * N_G, PENCIL, WIDE), ("blk_1", *GRP), 0, 0, tiled=True)
    key_grad, value_grad = placed_out(keys_out_kernel, dkv.reshape(N_Z, N_G, HALF, WIDE), 2, "keys_out")
    (query_grad,) = placed_out(queries_out_kernel, dq.reshape(N_Y, N_G, PENCIL, WIDE), 1, "queries_out")
    return query_grad, key_grad, value_grad


def solution(mesh):
    split = Mesh(mesh.devices.reshape(4, 2, 2, 4, 2), BLK_GRP)
    return jax.shard_map(
        on_device,
        mesh=split,
        in_specs=(P(BLK_GRP, None), P(BLK_GRP, None), P(GRP, None), P(GRP, None), P()),
        out_specs=(P(BLK_GRP, None), P(BLK_GRP, None), P(BLK_GRP, None)),
        check_vma=False,
    )
```

```python
import functools
import math

import jax
import jax.numpy as jnp
from jax import lax
from jax.experimental import pallas as pl
from jax.experimental.pallas import tpu as pltpu
from jax.sharding import Mesh
from jax.sharding import PartitionSpec as P


D = 1536
H = 16
HD = D // H
PENCIL = 16
PD = 64
HALF = PD // 2
WIDE = 4 * HD
N_Z = 4
N_Y = 2
N_G = 16
GRP = ("grp_0", "grp_1", "grp_2")
BLK_GRP = ("blk_0", "blk_1", "grp_0", "grp_1", "grp_2")
SCALE = 1.0 / math.sqrt(HD)
C2 = SCALE * math.log2(math.e)
TQ = 1024
TK = 512
GUN = 1
STQ = 1024
STK = 2048
SUB = 64
SUN = 1
CHUNKS = 2
NEG = -1e30
F32 = jnp.float32
BF16 = jnp.bfloat16
CONTRACT_LAST = (((1,), (1,)), ((), ()))
CONTRACT_FIRST = (((0,), (0,)), ((), ()))


def mm(a, b, dims=(((1,), (0,)), ((), ()))):
    return lax.dot_general(a, b, dims, preferred_element_type=F32)


KR = N_Z * HALF
SR = KR + HALF
PK = N_G * KR
PQ = N_G * HALF
WINDOWS = ((0, 128, 0), (0, 256, HD), (128, 256, 2 * HD - 128), (256, 128, 3 * HD - 256))


def shift(rows, cols, src, dst):
    i = lax.broadcasted_iota(jnp.int32, (rows, cols), 0) - src
    j = lax.broadcasted_iota(jnp.int32, (rows, cols), 1) - dst
    return jnp.where((i == j) & (i >= 0) & (i < HD), 1.0, 0.0).astype(BF16)


def turned_shift(cols, src):
    i = lax.broadcasted_iota(jnp.int32, (128, cols), 0)
    j = lax.broadcasted_iota(jnp.int32, (128, cols), 1) - src
    return jnp.where((i == j) & (i < HD), 1.0, 0.0).astype(BF16)


def pack_four(parts):
    a, b, c, d = parts
    return (
        (a + b[:, :128]).astype(BF16),
        (b[:, 128:] + c[:, :128]).astype(BF16),
        (c[:, 128:] + d).astype(BF16),
    )


def pack_kernel(order_ref, place_ref, q_ref, g_ref, k_ref, v_ref, out_ref, ka_s, va_s, kb_s, vb_s):
    y = place_ref[0]
    g = place_ref[1]
    for zt in range(N_Z):
        for part in range(PD // PENCIL):
            target = ((zt * N_Y + y) * N_G + g) * (PD // PENCIL) + part
            start = pl.multiple_of((order_ref[target] - g * (N_Z * N_Y * PD // PENCIL)) * PENCIL, PENCIL)
            row = zt * HALF + part % 2 * PENCIL
            k_s, v_s = ((ka_s, va_s), (kb_s, vb_s))[part // 2]
            k_s[row : row + PENCIL, :] = k_ref[pl.ds(start, PENCIL), :]
            v_s[row : row + PENCIL, :] = v_ref[pl.ds(start, PENCIL), :]
    for half, (k_s, v_s) in enumerate(((ka_s, va_s), (kb_s, vb_s))):
        k_s[KR:SR, :] = q_ref[half * HALF : (half + 1) * HALF, :]
        v_s[KR:SR, :] = g_ref[half * HALF : (half + 1) * HALF, :]
    for turn in range(4):
        heads = range(turn, H, 4)
        offset = turn * HD % 128
        width = 128 if offset + HD <= 128 else 256
        parts = []
        for ref, (_, cols, dst) in zip((ka_s, va_s, kb_s, vb_s), WINDOWS):
            x = jnp.concatenate([ref[:, h * HD // 128 * 128 : h * HD // 128 * 128 + width] for h in heads], axis=0)
            parts.append(mm(x, shift(width, cols, offset, dst)))
        for n, piece in enumerate(pack_four(parts)):
            for k, h in enumerate(heads):
                out_ref[h, :, n * 128 : (n + 1) * 128] = piece[k * SR : (k + 1) * SR]


def pack(order, place, obj_query, grad_out, pattern_key, pattern_value):
    vmem = pl.BlockSpec(memory_space=pltpu.VMEM)
    return pl.pallas_call(
        pack_kernel,
        out_shape=jax.ShapeDtypeStruct((H, SR, WIDE), BF16),
        in_specs=[pl.BlockSpec(memory_space=pltpu.SMEM), pl.BlockSpec(memory_space=pltpu.SMEM), vmem, vmem, vmem, vmem],
        out_specs=vmem,
        scratch_shapes=[pltpu.VMEM((SR, D), BF16)] * 4,
        name="pack",
    )(order, place, obj_query, grad_out, pattern_key, pattern_value)


def unpack(read, rows, stores):
    for (start, width, offset), (ref, base) in zip(WINDOWS, stores):
        ref[base : base + rows, :] = mm(read(slice(start, start + width)), shift(width, 128, offset, 0)).astype(BF16)


def unpack_keys(kv_ref, k_s, v_s, chunk, chunks, t_s=None):
    rows = HALF // chunks
    for zt in range(N_Z):
        at = slice(zt * HALF + chunk * rows, zt * HALF + (chunk + 1) * rows)
        k_first, k_second = zt * N_G * rows, (N_Z + zt) * N_G * rows

        def read(lanes):
            return kv_ref[:, at, lanes].reshape(N_G * rows, lanes.stop - lanes.start)

        unpack(read, N_G * rows, ((k_s, k_first), (v_s, k_first), (k_s, k_second), (v_s, k_second)))
        if t_s is not None:
            for (start, width, offset), base in ((WINDOWS[0], k_first), (WINDOWS[2], k_second)):
                x = read(slice(start, start + width))
                t_s[:, base : base + N_G * rows] = mm(turned_shift(width, offset), x, CONTRACT_LAST)[:HD].astype(BF16)


def unpack_turned(read, rows, stores):
    for (start, width, offset), (ref, base) in zip(WINDOWS, stores):
        x = read(slice(start, start + width))
        ref[:, base : base + rows] = mm(turned_shift(width, offset), x, CONTRACT_LAST).astype(BF16)


def unpack_queries(q_ref, q_s, g_s, base):
    unpack_turned(
        lambda lanes: q_ref[:, :, lanes].reshape(PQ, lanes.stop - lanes.start),
        PQ,
        ((q_s, base), (g_s, base), (q_s, base + PQ), (g_s, base + PQ)),
    )


def unpack_query_rows(q_ref, q_s, g_s, base):
    unpack(
        lambda lanes: q_ref[:, :, lanes].reshape(PQ, lanes.stop - lanes.start),
        PQ,
        ((q_s, base), (g_s, base), (q_s, base + PQ), (g_s, base + PQ)),
    )


def stats_kernel(q_ref, kv_ref, st_ref, q_s, g_s, k_s, v_s):
    unpack_keys(kv_ref, k_s, v_s, 0, 1)
    unpack_queries(q_ref, q_s, g_s, 0)

    def one_tile(t, _):
        q0 = pl.multiple_of(t * STQ, STQ)
        qt = q_s[:, pl.ds(q0, STQ)]
        gt = g_s[:, pl.ds(q0, STQ)]

        def one_chunk(j, carry):
            m, l, w = carry
            k0 = pl.multiple_of(j * STK, STK)
            s = mm(k_s[pl.ds(k0, STK), :], qt).reshape(STK // SUB, SUB // 8, 8, STQ)
            d = mm(v_s[pl.ds(k0, STK), :], gt).reshape(STK // SUB, SUB // 8, 8, STQ)
            for n in range(STK // SUB):
                top = jnp.maximum(m, jnp.max(s[n], axis=0))
                fade = jnp.exp2((m - top) * C2)
                e = jnp.exp2((s[n] - top[None]) * C2)
                m, l, w = top, l * fade + jnp.sum(e, axis=0), w * fade + jnp.sum(e * d[n], axis=0)
            return m, l, w

        zero = jnp.zeros((8, STQ), F32)
        m, l, w = lax.fori_loop(0, 2 * PK // STK, one_chunk, (jnp.full((8, STQ), NEG, F32), zero, zero), unroll=SUN)
        top = jnp.max(m, axis=0, keepdims=True)
        fade = jnp.exp2((m - top) * C2)
        st_ref[0:1, pl.ds(q0, STQ)] = top
        st_ref[1:2, pl.ds(q0, STQ)] = jnp.sum(l * fade, axis=0, keepdims=True)
        st_ref[2:3, pl.ds(q0, STQ)] = jnp.sum(w * fade, axis=0, keepdims=True)
        return 0

    lax.fori_loop(0, 2 * PQ // STQ, one_tile, 0)
    st_ref[3:8, :] = jnp.zeros((5, 2 * PQ), F32)


def stats(q, kv):
    vmem = pl.BlockSpec(memory_space=pltpu.VMEM)
    return pl.pallas_call(
        stats_kernel,
        out_shape=jax.ShapeDtypeStruct((8, 2 * PQ), F32),
        in_specs=[vmem, vmem],
        out_specs=vmem,
        scratch_shapes=[pltpu.VMEM((128, 2 * PQ), BF16)] * 2 + [pltpu.VMEM((2 * PK, 128), BF16)] * 2,
        cost_estimate=pl.CostEstimate(
            flops=4 * 2 * PQ * 2 * PK * 256, transcendentals=2 * PQ * 2 * PK, bytes_accessed=4 << 20
        ),
        name="stats",
    )(q, kv)


def joined(mine, theirs):
    top = jnp.maximum(mine[0:1], theirs[0:1])
    a = jnp.exp2((mine[0:1] - top) * C2)
    b = jnp.exp2((theirs[0:1] - top) * C2)
    total = mine[1:2] * a + theirs[1:2] * b
    return top * C2 + jnp.log2(total), (mine[2:3] * a + theirs[2:3] * b) / total


def grads_kernel(chunk, place_ref, qa_ref, qb_ref, kv_ref, sa_ref, sb_ref, ta_ref, tb_ref, *refs):
    first, last = chunk == 0, chunk == CHUNKS - 1
    so_far_ref = None if first else refs[0]
    dq_ref, dkv_ref, q_s, g_s, k_s, v_s, t_s, dq_s, dk_s, dv_s, log_s, mean_s = refs[0 if first else 1 :]
    if not last:
        dq_s = dq_ref
    unpack_keys(kv_ref, k_s, v_s, chunk, CHUNKS, t_s)
    unpack_query_rows(qa_ref, q_s, g_s, 0)
    unpack_query_rows(qb_ref, q_s, g_s, 2 * PQ)
    for n, (mine, theirs) in enumerate(((sa_ref, tb_ref), (sb_ref, ta_ref))):
        log_now, mean_now = joined(mine, theirs)
        log_s[:, n * 2 * PQ : (n + 1) * 2 * PQ] = jnp.broadcast_to(log_now, (8, 2 * PQ))
        mean_s[:, n * 2 * PQ : (n + 1) * 2 * PQ] = jnp.broadcast_to(mean_now, (8, 2 * PQ))
    dq_s[...] = jnp.zeros_like(dq_s) if first else so_far_ref[...]

    def one_chunk(j, _):
        k0 = pl.multiple_of(j * TK, TK)
        kc = k_s[pl.ds(k0, TK), :]
        vc = v_s[pl.ds(k0, TK), :]
        kt = t_s[:, pl.ds(k0, TK)]

        def one_tile(t, carry):
            dk, dv = carry
            q0 = pl.multiple_of(t * TQ, TQ)
            qt = q_s[pl.ds(q0, TQ), :]
            gt = g_s[pl.ds(q0, TQ), :]
            s = mm(kc, qt, CONTRACT_LAST).reshape(TK // 8, 8, TQ)
            d = mm(vc, gt, CONTRACT_LAST).reshape(TK // 8, 8, TQ)
            p = jnp.exp2(s * C2 - log_s[:, pl.ds(q0, TQ)][None])
            sg = ((d - mean_s[:, pl.ds(q0, TQ)][None]) * (p * SCALE)).astype(BF16).reshape(TK, TQ)
            p = p.astype(BF16).reshape(TK, TQ)
            dq_s[:, pl.ds(q0, TQ)] += mm(kt, sg)
            return dk + mm(sg, qt), dv + mm(p, gt)

        zero = jnp.zeros((TK, 128), F32)
        dk, dv = lax.fori_loop(0, 4 * PQ // TQ, one_tile, (zero, zero), unroll=GUN)
        dk_s[pl.ds(k0, TK), :] = dk.astype(BF16)
        dv_s[pl.ds(k0, TK), :] = dv.astype(BF16)
        return 0

    lax.fori_loop(0, 2 * PK // CHUNKS // TK, one_chunk, 0)
    place4 = [shift(HD, cols, 0, dst) for _, cols, dst in WINDOWS]
    rows = PK // CHUNKS
    parts = [
        mm(ref[half * rows : (half + 1) * rows, :HD], place4[n])
        for n, (ref, half) in enumerate(((dk_s, 0), (dv_s, 0), (dk_s, 1), (dv_s, 1)))
    ]
    for n, piece in enumerate(pack_four(parts)):
        dkv_ref[:, :, n * 128 : (n + 1) * 128] = piece.reshape(N_Z * N_G, HALF // CHUNKS, 128)
    if last:
        y = place_ref[0]
        for n, where in enumerate((y, 1 - y)):
            parts = []
            for quarter in range(4):
                r0 = n * 2 * PQ + quarter // 2 * PQ
                x = mm(dq_s[:, r0 : r0 + PQ].astype(BF16), place4[quarter], CONTRACT_FIRST)
                x = x.reshape(N_G, 2, PENCIL, x.shape[1])[:, quarter % 2]
                parts.append(x.reshape(N_G * PENCIL, x.shape[2]))
            for k, piece in enumerate(pack_four(parts)):
                dq_ref[where, :, :, k * 128 : (k + 1) * 128] = piece.reshape(N_G, PENCIL, 128)


def grads(chunk, place, qa, qb, kv, sa, sb, ta, tb, *so_far):
    vmem = pl.BlockSpec(memory_space=pltpu.VMEM)
    last = chunk == CHUNKS - 1
    return pl.pallas_call(
        functools.partial(grads_kernel, chunk),
        out_shape=(
            jax.ShapeDtypeStruct((N_Y, N_G, PENCIL, WIDE), BF16) if last else jax.ShapeDtypeStruct((HD, 4 * PQ), F32),
            jax.ShapeDtypeStruct((N_Z * N_G, HALF // CHUNKS, WIDE), BF16),
        ),
        in_specs=[pl.BlockSpec(memory_space=pltpu.SMEM)] + [vmem] * (7 + len(so_far)),
        out_specs=(vmem, vmem),
        scratch_shapes=[pltpu.VMEM((4 * PQ, 128), BF16)] * 2
        + [pltpu.VMEM((2 * PK // CHUNKS, 128), BF16)] * 2
        + [pltpu.VMEM((HD, 2 * PK // CHUNKS), BF16)]
        + [pltpu.VMEM((HD, 4 * PQ) if last else (8, 128), F32)]
        + [pltpu.VMEM((2 * PK // CHUNKS, 128), BF16)] * 2
        + [pltpu.VMEM((8, 4 * PQ), F32)] * 2,
        cost_estimate=pl.CostEstimate(
            flops=10 * 4 * PQ * 2 * PK * 128 // CHUNKS * 2,
            transcendentals=4 * PQ * 2 * PK // CHUNKS,
            bytes_accessed=8 << 20,
        ),
        name="grads",
    )(place, qa, qb, kv, sa, sb, ta, tb, *so_far)


def keys_out_kernel(*refs):
    key_ref, value_ref = refs[CHUNKS:]
    size = HALF // CHUNKS
    for n, got_ref in enumerate(refs[:CHUNKS]):
        for h in range(H):
            total = got_ref[0, h].astype(F32)
            for z in range(1, N_Z):
                total = total + got_ref[z, h].astype(F32)
            total = total.astype(BF16)
            for half in range(2):
                lane = half * 2 * HD
                rows = slice(half * HALF + n * size, half * HALF + (n + 1) * size)
                key_ref[rows, h * HD : (h + 1) * HD] = total[:, lane : lane + HD]
                value_ref[rows, h * HD : (h + 1) * HD] = total[:, lane + HD : lane + 2 * HD]


def queries_out_kernel(got_ref, query_ref):
    for h in range(H):
        total = (got_ref[0, h].astype(F32) + got_ref[1, h].astype(F32)).astype(BF16)
        for quarter in range(4):
            rows = slice(quarter * PENCIL, (quarter + 1) * PENCIL)
            query_ref[rows, h * HD : (h + 1) * HD] = total[:, quarter * HD : (quarter + 1) * HD]


def placed_out(kernel, got, outs):
    vmem = pl.BlockSpec(memory_space=pltpu.VMEM)
    return pl.pallas_call(
        kernel,
        out_shape=[jax.ShapeDtypeStruct((PD, D), BF16)] * outs,
        in_specs=[vmem] * len(got),
        out_specs=[vmem] * outs,
    )(*got)


def layer(obj_query, grad_out, pattern_key, pattern_value, pencil_order):
    place = jnp.stack([lax.axis_index("blk_1"), lax.axis_index(GRP)]).astype(jnp.int32)
    swap = functools.partial(lax.ppermute, axis_name="blk_1", perm=((0, 1), (1, 0)))
    sent = pack(pencil_order, place, obj_query, grad_out, pattern_key, pattern_value)
    got = lax.all_to_all(sent, GRP, 0, 0, tiled=True)
    qa = got[:, KR:, :]
    qb = swap(qa)
    sa = stats(qa, got)
    ta = swap(sa)
    sb = stats(qb, got)
    tb = swap(sb)
    so_far, pieces = (), []
    for chunk in range(CHUNKS):
        dq, dkv = grads(chunk, place, qa, qb, got, sa, sb, ta, tb, *so_far)
        so_far = (dq,)
        dkv = lax.all_to_all(dkv, ("blk_0", *GRP), 0, 0, tiled=True)
        pieces.append(dkv.reshape(N_Z, N_G, HALF // CHUNKS, WIDE))
    dq = lax.all_to_all(dq.reshape(N_Y * N_G, PENCIL, WIDE), ("blk_1", *GRP), 0, 0, tiled=True)
    (query_grad,) = placed_out(queries_out_kernel, [dq.reshape(N_Y, N_G, PENCIL, WIDE)], 1)
    key_grad, value_grad = placed_out(keys_out_kernel, pieces, 2)
    return query_grad, key_grad, value_grad


def solution(mesh):
    split = Mesh(mesh.devices.reshape(4, 2, 2, 4, 2), BLK_GRP)
    return jax.shard_map(
        layer,
        mesh=split,
        in_specs=(P(BLK_GRP, None), P(BLK_GRP, None), P(GRP, None), P(GRP, None), P()),
        out_specs=(P(BLK_GRP, None), P(BLK_GRP, None), P(BLK_GRP, None)),
        check_vma=False,
    )
```

```python
import functools
import math

import jax
import jax.numpy as jnp
from jax import lax
from jax.experimental import pallas as pl
from jax.experimental.pallas import tpu as pltpu
from jax.sharding import Mesh
from jax.sharding import PartitionSpec as P


D = 1536
H = 16
HD = D // H
PENCIL = 16
PD = 64
HALF = PD // 2
WIDE = 4 * HD
N_Z = 4
N_Y = 2
N_G = 16
GRP = ("grp_0", "grp_1", "grp_2")
HEADS = ("blk_1", "grp_0", "grp_1")
Z = "blk_0"
CORE = "grp_2"
BLK_GRP = ("blk_0", "blk_1", "grp_0", "grp_1", "grp_2")
SCALE = 1.0 / math.sqrt(HD)
C2 = SCALE * math.log2(math.e)
TQ = 1024
TK = 512
GUN = 1
STQ = 1024
STK = 2048
SUB = 64
SUN = 1
CHUNKS = 2
NEG = -1e30
F32 = jnp.float32
BF16 = jnp.bfloat16
CONTRACT_LAST = (((1,), (1,)), ((), ()))
CONTRACT_FIRST = (((0,), (0,)), ((), ()))


def mm(a, b, dims=(((1,), (0,)), ((), ()))):
    return lax.dot_general(a, b, dims, preferred_element_type=F32)


KR = N_Z * HALF
SR = KR + HALF
PK = N_G * KR
PQ = N_G * HALF
WINDOWS = ((0, 128, 0), (0, 256, HD), (128, 256, 2 * HD - 128), (256, 128, 3 * HD - 256))


def shift(rows, cols, src, dst):
    i = lax.broadcasted_iota(jnp.int32, (rows, cols), 0) - src
    j = lax.broadcasted_iota(jnp.int32, (rows, cols), 1) - dst
    return jnp.where((i == j) & (i >= 0) & (i < HD), 1.0, 0.0).astype(BF16)


def turned_shift(cols, src):
    i = lax.broadcasted_iota(jnp.int32, (128, cols), 0)
    j = lax.broadcasted_iota(jnp.int32, (128, cols), 1) - src
    return jnp.where((i == j) & (i < HD), 1.0, 0.0).astype(BF16)


def pack_four(parts):
    a, b, c, d = parts
    return (
        (a + b[:, :128]).astype(BF16),
        (b[:, 128:] + c[:, :128]).astype(BF16),
        (c[:, 128:] + d).astype(BF16),
    )


def pack_kernel(order_ref, place_ref, q_ref, g_ref, k_ref, v_ref, out_ref, ka_s, va_s, kb_s, vb_s):
    y = place_ref[0]
    g = place_ref[1]
    for zt in range(N_Z):
        for part in range(PD // PENCIL):
            target = ((zt * N_Y + y) * N_G + g) * (PD // PENCIL) + part
            start = pl.multiple_of((order_ref[target] - g * (N_Z * N_Y * PD // PENCIL)) * PENCIL, PENCIL)
            row = zt * HALF + part % 2 * PENCIL
            k_s, v_s = ((ka_s, va_s), (kb_s, vb_s))[part // 2]
            k_s[row : row + PENCIL, :] = k_ref[pl.ds(start, PENCIL), :]
            v_s[row : row + PENCIL, :] = v_ref[pl.ds(start, PENCIL), :]
    for half, (k_s, v_s) in enumerate(((ka_s, va_s), (kb_s, vb_s))):
        k_s[KR:SR, :] = q_ref[half * HALF : (half + 1) * HALF, :]
        v_s[KR:SR, :] = g_ref[half * HALF : (half + 1) * HALF, :]
    for turn in range(4):
        heads = range(turn, H, 4)
        offset = turn * HD % 128
        width = 128 if offset + HD <= 128 else 256
        parts = []
        for ref, (_, cols, dst) in zip((ka_s, va_s, kb_s, vb_s), WINDOWS):
            x = jnp.concatenate([ref[:, h * HD // 128 * 128 : h * HD // 128 * 128 + width] for h in heads], axis=0)
            parts.append(mm(x, shift(width, cols, offset, dst)))
        for n, piece in enumerate(pack_four(parts)):
            for k, h in enumerate(heads):
                out_ref[h, :, n * 128 : (n + 1) * 128] = piece[k * SR : (k + 1) * SR]


def pack(order, place, obj_query, grad_out, pattern_key, pattern_value):
    vmem = pl.BlockSpec(memory_space=pltpu.VMEM)
    return pl.pallas_call(
        pack_kernel,
        out_shape=jax.ShapeDtypeStruct((H, SR, WIDE), BF16),
        in_specs=[pl.BlockSpec(memory_space=pltpu.SMEM), pl.BlockSpec(memory_space=pltpu.SMEM), vmem, vmem, vmem, vmem],
        out_specs=vmem,
        scratch_shapes=[pltpu.VMEM((SR, D), BF16)] * 4,
        name="pack",
    )(order, place, obj_query, grad_out, pattern_key, pattern_value)


def unpack(read, rows, stores):
    for (start, width, offset), (ref, base) in zip(WINDOWS, stores):
        ref[base : base + rows, :] = mm(read(slice(start, start + width)), shift(width, 128, offset, 0)).astype(BF16)


def unpack_keys(kv_ref, k_s, v_s, chunk, chunks, t_s=None):
    rows = HALF // chunks
    for zt in range(N_Z):
        at = slice(zt * HALF + chunk * rows, zt * HALF + (chunk + 1) * rows)
        k_first, k_second = zt * N_G * rows, (N_Z + zt) * N_G * rows

        def read(lanes):
            return kv_ref[:, at, lanes].reshape(N_G * rows, lanes.stop - lanes.start)

        unpack(read, N_G * rows, ((k_s, k_first), (v_s, k_first), (k_s, k_second), (v_s, k_second)))
        if t_s is not None:
            for (start, width, offset), base in ((WINDOWS[0], k_first), (WINDOWS[2], k_second)):
                x = read(slice(start, start + width))
                t_s[:, base : base + N_G * rows] = mm(turned_shift(width, offset), x, CONTRACT_LAST)[:HD].astype(BF16)


def unpack_turned(read, rows, stores):
    for (start, width, offset), (ref, base) in zip(WINDOWS, stores):
        x = read(slice(start, start + width))
        ref[:, base : base + rows] = mm(turned_shift(width, offset), x, CONTRACT_LAST).astype(BF16)


def unpack_queries(q_ref, q_s, g_s, base):
    unpack_turned(
        lambda lanes: q_ref[:, :, lanes].reshape(PQ, lanes.stop - lanes.start),
        PQ,
        ((q_s, base), (g_s, base), (q_s, base + PQ), (g_s, base + PQ)),
    )


def unpack_query_rows(q_ref, q_s, g_s, base):
    unpack(
        lambda lanes: q_ref[:, :, lanes].reshape(PQ, lanes.stop - lanes.start),
        PQ,
        ((q_s, base), (g_s, base), (q_s, base + PQ), (g_s, base + PQ)),
    )


def stats_kernel(qa_ref, qb_ref, kv_ref, st_ref, q_s, g_s, k_s, v_s):
    unpack_keys(kv_ref, k_s, v_s, 0, 1)
    unpack_queries(qa_ref, q_s, g_s, 0)
    unpack_queries(qb_ref, q_s, g_s, 2 * PQ)

    def one_tile(t, _):
        q0 = pl.multiple_of(t * STQ, STQ)
        qt = q_s[:, pl.ds(q0, STQ)]
        gt = g_s[:, pl.ds(q0, STQ)]

        def one_chunk(j, carry):
            m, l, w = carry
            k0 = pl.multiple_of(j * STK, STK)
            s = mm(k_s[pl.ds(k0, STK), :], qt).reshape(STK // SUB, SUB // 8, 8, STQ)
            d = mm(v_s[pl.ds(k0, STK), :], gt).reshape(STK // SUB, SUB // 8, 8, STQ)
            for n in range(STK // SUB):
                top = jnp.maximum(m, jnp.max(s[n], axis=0))
                fade = jnp.exp2((m - top) * C2)
                e = jnp.exp2((s[n] - top[None]) * C2)
                m, l, w = top, l * fade + jnp.sum(e, axis=0), w * fade + jnp.sum(e * d[n], axis=0)
            return m, l, w

        zero = jnp.zeros((8, STQ), F32)
        m, l, w = lax.fori_loop(0, 2 * PK // STK, one_chunk, (jnp.full((8, STQ), NEG, F32), zero, zero), unroll=SUN)
        top = jnp.max(m, axis=0, keepdims=True)
        fade = jnp.exp2((m - top) * C2)
        st_ref[0:1, pl.ds(q0, STQ)] = top
        st_ref[1:2, pl.ds(q0, STQ)] = jnp.sum(l * fade, axis=0, keepdims=True)
        st_ref[2:3, pl.ds(q0, STQ)] = jnp.sum(w * fade, axis=0, keepdims=True)
        return 0

    lax.fori_loop(0, 4 * PQ // STQ, one_tile, 0)
    st_ref[3:8, :] = jnp.zeros((5, 4 * PQ), F32)


def stats(qa, qb, kv):
    vmem = pl.BlockSpec(memory_space=pltpu.VMEM)
    return pl.pallas_call(
        stats_kernel,
        out_shape=jax.ShapeDtypeStruct((8, 4 * PQ), F32),
        in_specs=[vmem] * 3,
        out_specs=vmem,
        scratch_shapes=[pltpu.VMEM((128, 4 * PQ), BF16)] * 2 + [pltpu.VMEM((2 * PK, 128), BF16)] * 2,
        cost_estimate=pl.CostEstimate(
            flops=4 * 4 * PQ * 2 * PK * 256, transcendentals=4 * PQ * 2 * PK, bytes_accessed=4 << 20
        ),
        name="stats",
    )(qa, qb, kv)


def joined(mine, theirs):
    top = jnp.maximum(mine[0:1], theirs[0:1])
    a = jnp.exp2((mine[0:1] - top) * C2)
    b = jnp.exp2((theirs[0:1] - top) * C2)
    total = mine[1:2] * a + theirs[1:2] * b
    return top * C2 + jnp.log2(total), (mine[2:3] * a + theirs[2:3] * b) / total


def grads_kernel(chunk, place_ref, qa_ref, qb_ref, kv_ref, mine_ref, theirs_ref, *refs):
    first, last = chunk == 0, chunk == CHUNKS - 1
    so_far_ref = None if first else refs[0]
    refs = refs[0 if first else 1 :]
    dq_refs, dkv_refs = (refs[:2], refs[2:6]) if last else (refs[:1], refs[1:5])
    q_s, g_s, k_s, v_s, t_s, dq_s, dk_s, dv_s, log_s, mean_s, out_s = refs[6 if last else 5 :]
    if not last:
        dq_s = dq_refs[0]
    unpack_keys(kv_ref, k_s, v_s, chunk, CHUNKS, t_s)
    unpack_query_rows(qa_ref, q_s, g_s, 0)
    unpack_query_rows(qb_ref, q_s, g_s, 2 * PQ)
    for n in range(2):
        here, there = slice(n * 2 * PQ, (n + 1) * 2 * PQ), slice((1 - n) * 2 * PQ, (2 - n) * 2 * PQ)
        log_now, mean_now = joined(mine_ref[:, here], theirs_ref[:, there])
        log_s[:, here] = jnp.broadcast_to(log_now, (8, 2 * PQ))
        mean_s[:, here] = jnp.broadcast_to(mean_now, (8, 2 * PQ))
    dq_s[...] = jnp.zeros_like(dq_s) if first else so_far_ref[...]

    def one_chunk(j, _):
        k0 = pl.multiple_of(j * TK, TK)
        kc = k_s[pl.ds(k0, TK), :]
        vc = v_s[pl.ds(k0, TK), :]
        kt = t_s[:, pl.ds(k0, TK)]

        def one_tile(t, carry):
            dk, dv = carry
            q0 = pl.multiple_of(t * TQ, TQ)
            qt = q_s[pl.ds(q0, TQ), :]
            gt = g_s[pl.ds(q0, TQ), :]
            s = mm(kc, qt, CONTRACT_LAST).reshape(TK // 8, 8, TQ)
            d = mm(vc, gt, CONTRACT_LAST).reshape(TK // 8, 8, TQ)
            p = jnp.exp2(s * C2 - log_s[:, pl.ds(q0, TQ)][None])
            sg = ((d - mean_s[:, pl.ds(q0, TQ)][None]) * (p * SCALE)).astype(BF16).reshape(TK, TQ)
            p = p.astype(BF16).reshape(TK, TQ)
            dq_s[:, pl.ds(q0, TQ)] += mm(kt, sg)
            return dk + mm(sg, qt), dv + mm(p, gt)

        zero = jnp.zeros((TK, 128), F32)
        dk, dv = lax.fori_loop(0, 4 * PQ // TQ, one_tile, (zero, zero), unroll=GUN)
        dk_s[pl.ds(k0, TK), :] = dk.astype(BF16)
        dv_s[pl.ds(k0, TK), :] = dv.astype(BF16)
        return 0

    lax.fori_loop(0, 2 * PK // CHUNKS // TK, one_chunk, 0)
    place4 = [shift(HD, cols, 0, dst) for _, cols, dst in WINDOWS]
    rows = PK // CHUNKS
    parts = [
        mm(ref[half * rows : (half + 1) * rows, :HD], place4[n])
        for n, (ref, half) in enumerate(((dk_s, 0), (dv_s, 0), (dk_s, 1), (dv_s, 1)))
    ]
    for n, piece in enumerate(pack_four(parts)):
        out_s[:, :, n * 128 : (n + 1) * 128] = piece.reshape(N_Z, rows // N_Z, 128)
    z = place_ref[2]
    for step, ref in enumerate(dkv_refs):
        ref[...] = out_s[(z + step) % N_Z].reshape(N_G, HALF // CHUNKS, WIDE)
    if last:
        for n, ref in enumerate(dq_refs):
            parts = []
            for quarter in range(4):
                r0 = n * 2 * PQ + quarter // 2 * PQ
                x = mm(dq_s[:, r0 : r0 + PQ].astype(BF16), place4[quarter], CONTRACT_FIRST)
                x = x.reshape(N_G, 2, PENCIL, x.shape[1])[:, quarter % 2]
                parts.append(x.reshape(N_G * PENCIL, x.shape[2]))
            for k, piece in enumerate(pack_four(parts)):
                ref[:, :, k * 128 : (k + 1) * 128] = piece.reshape(N_G, PENCIL, 128)


def grads(chunk, place, qa, qb, kv, mine, theirs, *so_far):
    vmem = pl.BlockSpec(memory_space=pltpu.VMEM)
    last = chunk == CHUNKS - 1
    outs = [jax.ShapeDtypeStruct((N_G, HALF // CHUNKS, WIDE), BF16)] * N_Z
    if last:
        outs = [jax.ShapeDtypeStruct((N_G, PENCIL, WIDE), BF16)] * 2 + outs
    else:
        outs = [jax.ShapeDtypeStruct((HD, 4 * PQ), F32)] + outs
    return pl.pallas_call(
        functools.partial(grads_kernel, chunk),
        out_shape=outs,
        in_specs=[pl.BlockSpec(memory_space=pltpu.SMEM)] + [vmem] * (5 + len(so_far)),
        out_specs=[vmem] * len(outs),
        scratch_shapes=[pltpu.VMEM((4 * PQ, 128), BF16)] * 2
        + [pltpu.VMEM((2 * PK // CHUNKS, 128), BF16)] * 2
        + [pltpu.VMEM((HD, 2 * PK // CHUNKS), BF16)]
        + [pltpu.VMEM((HD, 4 * PQ) if last else (8, 128), F32)]
        + [pltpu.VMEM((2 * PK // CHUNKS, 128), BF16)] * 2
        + [pltpu.VMEM((8, 4 * PQ), F32)] * 2
        + [pltpu.VMEM((N_Z, N_G * HALF // CHUNKS, WIDE), BF16)],
        cost_estimate=pl.CostEstimate(
            flops=10 * 4 * PQ * 2 * PK * 128 // CHUNKS * 2,
            transcendentals=4 * PQ * 2 * PK // CHUNKS,
            bytes_accessed=8 << 20,
        ),
        name="grads",
    )(place, qa, qb, kv, mine, theirs, *so_far)


def combine_kernel(*refs):
    out_ref = refs[-1]
    row = 0
    for parts in [refs[n * N_Z : (n + 1) * N_Z] for n in range(CHUNKS)] + [refs[CHUNKS * N_Z : -1]]:
        total = parts[0][...].astype(F32)
        for part in parts[1:]:
            total = total + part[...].astype(F32)
        out_ref[:, row : row + total.shape[1], :] = total.astype(BF16)
        row += total.shape[1]


def combine(parts):
    vmem = pl.BlockSpec(memory_space=pltpu.VMEM)
    return pl.pallas_call(
        combine_kernel,
        out_shape=jax.ShapeDtypeStruct((N_G, HALF + PENCIL, WIDE), BF16),
        in_specs=[vmem] * len(parts),
        out_specs=vmem,
        name="combine",
    )(*parts)


def finish_kernel(got_ref, query_ref, key_ref, value_ref):
    for h in range(H):
        here = slice(h * HD, (h + 1) * HD)
        for half in range(2):
            lane = half * 2 * HD
            rows = slice(half * HALF, (half + 1) * HALF)
            key_ref[rows, here] = got_ref[h, :HALF, lane : lane + HD]
            value_ref[rows, here] = got_ref[h, :HALF, lane + HD : lane + 2 * HD]
        for quarter in range(4):
            rows = slice(quarter * PENCIL, (quarter + 1) * PENCIL)
            query_ref[rows, here] = got_ref[h, HALF:, quarter * HD : (quarter + 1) * HD]


def finish(got):
    vmem = pl.BlockSpec(memory_space=pltpu.VMEM)
    return pl.pallas_call(
        finish_kernel,
        out_shape=[jax.ShapeDtypeStruct((PD, D), BF16)] * 3,
        in_specs=[vmem],
        out_specs=[vmem] * 3,
        name="finish",
    )(got)


def layer(obj_query, grad_out, pattern_key, pattern_value, pencil_order):
    place = jnp.stack([lax.axis_index("blk_1"), lax.axis_index(GRP), lax.axis_index(Z)]).astype(jnp.int32)
    swap = functools.partial(lax.ppermute, axis_name=CORE, perm=((0, 1), (1, 0)))
    sent = pack(pencil_order, place, obj_query, grad_out, pattern_key, pattern_value)
    got = lax.all_to_all(sent, HEADS, 0, 0, tiled=True)
    qa = got[:, KR:, :]
    qb = swap(qa)
    mine = stats(qa, qb, got)
    theirs = swap(mine)
    so_far, parts = (), []
    for chunk in range(CHUNKS):
        outs = grads(chunk, place, qa, qb, got, mine, theirs, *so_far)
        so_far = (outs[0],)
        pieces = outs[-N_Z:]
        parts.append(pieces[0])
        for step in range(1, N_Z):
            perm = tuple((k, (k + step) % N_Z) for k in range(N_Z))
            parts.append(lax.ppermute(pieces[step], Z, perm))
    parts += [outs[0], swap(outs[1])]
    total = combine(parts)
    total = lax.all_to_all(total, HEADS, 0, 0, tiled=True)
    return tuple(finish(total))


def solution(mesh):
    split = Mesh(mesh.devices.reshape(4, 2, 2, 4, 2), BLK_GRP)
    return jax.shard_map(
        layer,
        mesh=split,
        in_specs=(P(BLK_GRP, None), P(BLK_GRP, None), P(GRP, None), P(GRP, None), P()),
        out_specs=(P(BLK_GRP, None), P(BLK_GRP, None), P(BLK_GRP, None)),
        check_vma=False,
    )
```

```python
import functools
import math

import jax
import jax.numpy as jnp
from jax import lax
from jax.experimental import pallas as pl
from jax.experimental.pallas import tpu as pltpu
from jax.sharding import Mesh
from jax.sharding import PartitionSpec as P


D = 1536
H = 16
HD = D // H
PENCIL = 16
PD = 64
HALF = PD // 2
WIDE = 4 * HD
N_Z = 4
N_G = 16
BLK_GRP = ("blk_0", "blk_1", "grp_0", "grp_1", "grp_2")
GRP = ("grp_0", "grp_1", "grp_2")
HEADS = ("blk_1", "grp_0", "grp_1")
Z = "blk_0"
CORE = "grp_2"
SCALE = 1.0 / math.sqrt(HD)
C2 = SCALE * math.log2(math.e)
TQ = 1024
TK = 512
GUN = 1
STQ = 1024
STK = 2048
SUB = 64
SUN = 1
NEG = -1e30
F32 = jnp.float32
BF16 = jnp.bfloat16
CONTRACT_LAST = (((1,), (1,)), ((), ()))
CONTRACT_FIRST = (((0,), (0,)), ((), ()))
ROWS = N_G * PD
NQ = N_Z * ROWS
NK = 2 * ROWS
VMEM = pl.BlockSpec(memory_space=pltpu.VMEM)

WINDOWS = ((0, 128, 0), (0, 256, HD), (128, 256, 2 * HD - 128), (256, 128, 3 * HD - 256))


def mm(a, b, dims=(((1,), (0,)), ((), ()))):
    return lax.dot_general(a, b, dims, preferred_element_type=F32)


def shift(rows, cols, src, dst):
    i = lax.broadcasted_iota(jnp.int32, (rows, cols), 0) - src
    j = lax.broadcasted_iota(jnp.int32, (rows, cols), 1) - dst
    return jnp.where((i == j) & (i >= 0) & (i < HD), 1.0, 0.0).astype(BF16)


def turned_shift(cols, src):
    i = lax.broadcasted_iota(jnp.int32, (128, cols), 0)
    j = lax.broadcasted_iota(jnp.int32, (128, cols), 1) - src
    return jnp.where((i == j) & (i < HD), 1.0, 0.0).astype(BF16)


def pack_four(parts):
    a, b, c, d = parts
    return (
        (a + b[:, :128]).astype(BF16),
        (b[:, 128:] + c[:, :128]).astype(BF16),
        (c[:, 128:] + d).astype(BF16),
    )


def pack_rows(a_ref, b_ref, out_ref):
    for turn in range(4):
        heads = range(turn, H, 4)
        offset = turn * HD % 128
        width = 128 if offset + HD <= 128 else 256
        parts = []
        for n, (_, cols, dst) in enumerate(WINDOWS):
            ref = (a_ref, b_ref)[n % 2]
            rows = slice(n // 2 * HALF, (n // 2 + 1) * HALF)
            x = jnp.concatenate([ref[rows, h * HD // 128 * 128 : h * HD // 128 * 128 + width] for h in heads], axis=0)
            parts.append(mm(x, shift(width, cols, offset, dst)))
        for n, piece in enumerate(pack_four(parts)):
            for k, h in enumerate(heads):
                out_ref[h, :, n * 128 : (n + 1) * 128] = piece[k * HALF : (k + 1) * HALF]


def pack_queries(obj_query, grad_out):
    return pl.pallas_call(
        pack_rows,
        out_shape=jax.ShapeDtypeStruct((H, HALF, WIDE), BF16),
        in_specs=[VMEM, VMEM],
        out_specs=VMEM,
        name="pack_queries",
    )(obj_query, grad_out)


def pack_keys_kernel(blocks_ref, k_ref, v_ref, out_ref, k_s, v_s):
    i = pl.program_id(0)
    at = pl.ds(pl.multiple_of(i * PENCIL, PENCIL), PENCIL)
    k_s[at, :] = k_ref[...]
    v_s[at, :] = v_ref[...]

    @pl.when(i == PD // PENCIL - 1)
    def _():
        pack_rows(k_s, v_s, out_ref)


def pack_keys(blocks, pattern_key, pattern_value):
    block = pl.BlockSpec((PENCIL, D), lambda i, blocks: (blocks[i], 0))
    return pl.pallas_call(
        pack_keys_kernel,
        out_shape=jax.ShapeDtypeStruct((H, HALF, WIDE), BF16),
        grid_spec=pltpu.PrefetchScalarGridSpec(
            num_scalar_prefetch=1,
            grid=(PD // PENCIL,),
            in_specs=[block, block],
            out_specs=pl.BlockSpec((H, HALF, WIDE), lambda i, blocks: (0, 0, 0)),
            scratch_shapes=[pltpu.VMEM((PD, D), BF16)] * 2,
        ),
        name="pack_keys",
    )(blocks, pattern_key, pattern_value)


def unpack(ref, stores, turned=False):
    half = ROWS // 2
    for n, (start, width, offset) in enumerate(WINDOWS):
        out, base = stores[n % 2]
        if out is None:
            continue
        at = slice(base + n // 2 * half, base + n // 2 * half + half)
        x = ref[:, :, start : start + width].reshape(half, width)
        if turned:
            out[:, at] = mm(turned_shift(width, offset), x, CONTRACT_LAST)[: out.shape[0]].astype(BF16)
        else:
            out[at, :] = mm(x, shift(width, 128, offset, 0)).astype(BF16)


def stats_kernel(*refs):
    q_refs, kv_refs = refs[:N_Z], refs[N_Z : N_Z + 2]
    st_ref, q_s, g_s, k_s, v_s = refs[N_Z + 2 :]
    for n, ref in enumerate(kv_refs):
        unpack(ref, ((k_s, n * ROWS), (v_s, n * ROWS)))
    for n, ref in enumerate(q_refs):
        unpack(ref, ((q_s, n * ROWS), (g_s, n * ROWS)), turned=True)
    st_ref[...] = jnp.zeros_like(st_ref)

    for n in range(NQ // STQ):
        q0 = n * STQ
        qt = q_s[:, q0 : q0 + STQ]
        gt = g_s[:, q0 : q0 + STQ]

        def one_chunk(j, carry):
            m, l, w = carry
            k0 = pl.multiple_of(j * STK, STK)
            s = mm(k_s[pl.ds(k0, STK), :], qt).reshape(STK // SUB, SUB // 8, 8, STQ)
            d = mm(v_s[pl.ds(k0, STK), :], gt).reshape(STK // SUB, SUB // 8, 8, STQ)
            for i in range(STK // SUB):
                top = jnp.maximum(m, jnp.max(s[i], axis=0))
                fade = jnp.exp2((m - top) * C2)
                e = jnp.exp2((s[i] - top[None]) * C2)
                m, l, w = top, l * fade + jnp.sum(e, axis=0), w * fade + jnp.sum(e * d[i], axis=0)
            return m, l, w

        zero = jnp.zeros((8, STQ), F32)
        start = (jnp.full((8, STQ), NEG, F32), zero, zero)
        m, l, w = lax.fori_loop(0, NK // STK, one_chunk, start, unroll=SUN)
        top = jnp.max(m, axis=0, keepdims=True)
        fade = jnp.exp2((m - top) * C2)
        row, cols = q0 // (NQ // 2) * 4, slice(q0 % (NQ // 2), q0 % (NQ // 2) + STQ)
        st_ref[row : row + 1, cols] = top
        st_ref[row + 1 : row + 2, cols] = jnp.sum(l * fade, axis=0, keepdims=True)
        st_ref[row + 2 : row + 3, cols] = jnp.sum(w * fade, axis=0, keepdims=True)


def stats(queries, keys):
    return pl.pallas_call(
        stats_kernel,
        out_shape=jax.ShapeDtypeStruct((8, NQ // 2), F32),
        in_specs=[VMEM] * (N_Z + 2),
        out_specs=VMEM,
        scratch_shapes=[pltpu.VMEM((128, NQ), BF16)] * 2 + [pltpu.VMEM((NK, 128), BF16)] * 2,
        cost_estimate=pl.CostEstimate(flops=4 * NQ * NK * 256, transcendentals=NQ * NK, bytes_accessed=4 << 20),
        name="stats",
    )(*queries, *keys)


def block_of(ref, n):
    row, col = n // 2 * 4, n % 2 * ROWS
    return [ref[row + i : row + i + 1, col : col + ROWS] for i in range(3)]


def joined(parts):
    top = functools.reduce(jnp.maximum, [part[0] for part in parts])
    fades = [jnp.exp2((part[0] - top) * C2) for part in parts]
    total = sum(part[1] * fade for part, fade in zip(parts, fades))
    weighted = sum(part[2] * fade for part, fade in zip(parts, fades))
    return top * C2 + jnp.log2(total), weighted / total


def grads_kernel(*refs):
    q_refs, kv_refs, st_refs = refs[:N_Z], refs[N_Z : N_Z + 2], refs[N_Z + 2 : 2 * N_Z + 2]
    outs, scratch = refs[2 * N_Z + 2 : 3 * N_Z + 4], refs[3 * N_Z + 4 :]
    dkv_refs, dq_refs = outs[:2], outs[2:]
    q_s, g_s, k_s, v_s, t_s, dq_s, dk_s, dv_s, log_s, mean_s = scratch
    for n, ref in enumerate(kv_refs):
        unpack(ref, ((k_s, n * ROWS), (v_s, n * ROWS)))
        unpack(ref, ((t_s, n * ROWS), (None, 0)), turned=True)
    for n, ref in enumerate(q_refs):
        unpack(ref, ((q_s, n * ROWS), (g_s, n * ROWS)))
        log_now, mean_now = joined([block_of(st, (n - t) % N_Z) for t, st in enumerate(st_refs)])
        here = slice(n * ROWS, (n + 1) * ROWS)
        log_s[:, here] = jnp.broadcast_to(log_now, (8, ROWS))
        mean_s[:, here] = jnp.broadcast_to(mean_now, (8, ROWS))
    dq_s[...] = jnp.zeros_like(dq_s)

    def one_chunk(j, _):
        k0 = pl.multiple_of(j * TK, TK)
        kc = k_s[pl.ds(k0, TK), :]
        vc = v_s[pl.ds(k0, TK), :]
        kt = t_s[:, pl.ds(k0, TK)]

        def one_tile(t, carry):
            dk, dv = carry
            q0 = pl.multiple_of(t * TQ, TQ)
            qt = q_s[pl.ds(q0, TQ), :]
            gt = g_s[pl.ds(q0, TQ), :]
            s = mm(kc, qt, CONTRACT_LAST).reshape(TK // 8, 8, TQ)
            d = mm(vc, gt, CONTRACT_LAST).reshape(TK // 8, 8, TQ)
            p = jnp.exp2(s * C2 - log_s[:, pl.ds(q0, TQ)][None])
            sg = ((d - mean_s[:, pl.ds(q0, TQ)][None]) * (p * SCALE)).astype(BF16).reshape(TK, TQ)
            p = p.astype(BF16).reshape(TK, TQ)
            dq_s[:, pl.ds(q0, TQ)] += mm(kt, sg)
            return dk + mm(sg, qt), dv + mm(p, gt)

        zero = jnp.zeros((TK, 128), F32)
        dk, dv = lax.fori_loop(0, NQ // TQ, one_tile, (zero, zero), unroll=GUN)
        dk_s[pl.ds(k0, TK), :] = dk.astype(BF16)
        dv_s[pl.ds(k0, TK), :] = dv.astype(BF16)
        return 0

    lax.fori_loop(0, NK // TK, one_chunk, 0)
    place4 = [shift(HD, cols, 0, dst) for _, cols, dst in WINDOWS]
    half = ROWS // 2
    for n, ref in enumerate(dkv_refs):
        base = n * ROWS
        parts = [
            mm((dk_s, dv_s)[i % 2][base + i // 2 * half : base + (i // 2 + 1) * half, :HD], place4[i]) for i in range(4)
        ]
        for k, piece in enumerate(pack_four(parts)):
            ref[:, :, k * 128 : (k + 1) * 128] = piece.reshape(N_G, HALF, 128)
    for n, ref in enumerate(dq_refs):
        parts = []
        for quarter in range(4):
            r0 = n * ROWS + quarter // 2 * half
            x = mm(dq_s[:, r0 : r0 + half].astype(BF16), place4[quarter], CONTRACT_FIRST)
            x = x.reshape(N_G, 2, PENCIL, x.shape[1])[:, quarter % 2]
            parts.append(x.reshape(N_G * PENCIL, x.shape[2]))
        for k, piece in enumerate(pack_four(parts)):
            ref[:, :, k * 128 : (k + 1) * 128] = piece.reshape(N_G, PENCIL, 128)


def grads(queries, keys, statistics):
    return pl.pallas_call(
        grads_kernel,
        out_shape=[jax.ShapeDtypeStruct((N_G, HALF, WIDE), BF16)] * 2
        + [jax.ShapeDtypeStruct((N_G, PENCIL, WIDE), BF16)] * N_Z,
        in_specs=[VMEM] * (2 * N_Z + 2),
        out_specs=[VMEM] * (N_Z + 2),
        scratch_shapes=[pltpu.VMEM((NQ, 128), BF16)] * 2
        + [pltpu.VMEM((NK, 128), BF16)] * 2
        + [pltpu.VMEM((HD, NK), BF16)]
        + [pltpu.VMEM((HD, NQ), F32)]
        + [pltpu.VMEM((NK, 128), BF16)] * 2
        + [pltpu.VMEM((8, NQ), F32)] * 2,
        cost_estimate=pl.CostEstimate(flops=10 * NQ * NK * 256, transcendentals=NQ * NK, bytes_accessed=8 << 20),
        name="grads",
    )(*queries, *keys, *statistics)


def combine_kernel(*refs):
    out_ref = refs[-1]
    row = 0
    for parts in (refs[:2], refs[2:-1]):
        total = parts[0][...].astype(F32)
        for part in parts[1:]:
            total = total + part[...].astype(F32)
        out_ref[:, row : row + total.shape[1], :] = total.astype(BF16)
        row += total.shape[1]


def combine(parts):
    return pl.pallas_call(
        combine_kernel,
        out_shape=jax.ShapeDtypeStruct((N_G, HALF + PENCIL, WIDE), BF16),
        in_specs=[VMEM] * len(parts),
        out_specs=VMEM,
        name="combine",
    )(*parts)


def finish_kernel(got_ref, query_ref, key_ref, value_ref):
    for h in range(H):
        here = slice(h * HD, (h + 1) * HD)
        for half in range(2):
            lane = half * 2 * HD
            rows = slice(half * HALF, (half + 1) * HALF)
            key_ref[rows, here] = got_ref[h, :HALF, lane : lane + HD]
            value_ref[rows, here] = got_ref[h, :HALF, lane + HD : lane + 2 * HD]
        for quarter in range(4):
            rows = slice(quarter * PENCIL, (quarter + 1) * PENCIL)
            query_ref[rows, here] = got_ref[h, HALF:, quarter * HD : (quarter + 1) * HD]


def finish(got):
    return pl.pallas_call(
        finish_kernel,
        out_shape=[jax.ShapeDtypeStruct((PD, D), BF16)] * 3,
        in_specs=[VMEM],
        out_specs=[VMEM] * 3,
        name="finish",
    )(got)


def along_z(x, step):
    return lax.ppermute(x, Z, tuple((k, (k + step) % N_Z) for k in range(N_Z)))


def swapped(x):
    return lax.ppermute(x, CORE, ((0, 1), (1, 0)))


def to_heads(x):
    return lax.all_to_all(x, HEADS, 0, 0, tiled=True)


def layer(obj_query, grad_out, pattern_key, pattern_value, pencil_order):
    per_device = PD // PENCIL
    first = lax.axis_index(BLK_GRP) * per_device
    blocks = lax.dynamic_slice(pencil_order, (first,), (per_device,)) - lax.axis_index(GRP) * (pattern_key.shape[0] // PENCIL)
    queries = pack_queries(obj_query, grad_out)
    queries = [to_heads(queries)]
    keys = pack_keys(blocks, pattern_key, pattern_value)
    for step in range(1, N_Z):
        queries.append(along_z(queries[0], step))
    keys = [to_heads(keys)]
    keys.append(swapped(keys[0]))
    statistics = [stats(queries, keys)]
    for step in range(1, N_Z):
        statistics.append(along_z(statistics[0], step))
    outs = grads(queries, keys, statistics)
    parts = [outs[0], None, outs[2]]
    for step in range(1, N_Z):
        parts.append(along_z(outs[2 + step], N_Z - step))
    parts[1] = swapped(outs[1])
    total = combine(parts)
    total = to_heads(total)
    return tuple(finish(total))


def solution(mesh):
    split = Mesh(mesh.devices.reshape(4, 2, 2, 4, 2), BLK_GRP)
    return jax.shard_map(
        layer,
        mesh=split,
        in_specs=(P(BLK_GRP, None), P(BLK_GRP, None), P(GRP, None), P(GRP, None), P()),
        out_specs=(P(BLK_GRP, None), P(BLK_GRP, None), P(BLK_GRP, None)),
        check_vma=False,
    )
```

```python
import functools
import math

import jax
import jax.numpy as jnp
from jax import lax
from jax.experimental import pallas as pl
from jax.experimental.pallas import tpu as pltpu
from jax.sharding import Mesh
from jax.sharding import PartitionSpec as P


D = 1536
H = 16
HD = D // H
PENCIL = 16
PD = 64
HALF = PD // 2
WIDE = 4 * HD
N_Z = 4
N_G = 16
BLK_GRP = ("blk_0", "blk_1", "grp_0", "grp_1", "grp_2")
GRP = ("grp_0", "grp_1", "grp_2")
HEADS = ("blk_1", "grp_0", "grp_1")
Z = "blk_0"
CORE = "grp_2"
SCALE = 1.0 / math.sqrt(HD)
C2 = SCALE * math.log2(math.e)
TQ = 1024
TK = 512
GUN = 1
STQ = 1024
STK = 2048
SUB = 64
SUN = 1
NEG = -1e30
F32 = jnp.float32
BF16 = jnp.bfloat16
CONTRACT_LAST = (((1,), (1,)), ((), ()))
CONTRACT_FIRST = (((0,), (0,)), ((), ()))
ROWS = N_G * PD
NQ = N_Z * ROWS
NK = 2 * ROWS
VMEM = pl.BlockSpec(memory_space=pltpu.VMEM)

WINDOWS = ((0, 128, 0), (0, 256, HD), (128, 256, 2 * HD - 128), (256, 128, 3 * HD - 256))


def mm(a, b, dims=(((1,), (0,)), ((), ()))):
    return lax.dot_general(a, b, dims, preferred_element_type=F32)


def shift(rows, cols, src, dst):
    i = lax.broadcasted_iota(jnp.int32, (rows, cols), 0) - src
    j = lax.broadcasted_iota(jnp.int32, (rows, cols), 1) - dst
    return jnp.where((i == j) & (i >= 0) & (i < HD), 1.0, 0.0).astype(BF16)


def turned_shift(cols, src):
    i = lax.broadcasted_iota(jnp.int32, (128, cols), 0)
    j = lax.broadcasted_iota(jnp.int32, (128, cols), 1) - src
    return jnp.where((i == j) & (i < HD), 1.0, 0.0).astype(BF16)


def pack_four(parts):
    a, b, c, d = parts
    return (
        (a + b[:, :128]).astype(BF16),
        (b[:, 128:] + c[:, :128]).astype(BF16),
        (c[:, 128:] + d).astype(BF16),
    )


def pack_rows(a_ref, b_ref, out_ref, base):
    for turn in range(4):
        heads = range(turn, H, 4)
        offset = turn * HD % 128
        width = 128 if offset + HD <= 128 else 256
        parts = []
        for n, (_, cols, dst) in enumerate(WINDOWS):
            ref = (a_ref, b_ref)[n % 2]
            rows = slice(n // 2 * HALF, (n // 2 + 1) * HALF)
            x = jnp.concatenate([ref[rows, h * HD // 128 * 128 : h * HD // 128 * 128 + width] for h in heads], axis=0)
            parts.append(mm(x, shift(width, cols, offset, dst)))
        for n, piece in enumerate(pack_four(parts)):
            for k, h in enumerate(heads):
                out_ref[h, base : base + HALF, n * 128 : (n + 1) * 128] = piece[k * HALF : (k + 1) * HALF]


def pack_kernel(order_ref, place_ref, q_ref, g_ref, k_ref, v_ref, out_ref, k_s, v_s):
    i = pl.program_id(0)
    at = pl.ds(pl.multiple_of(i * PENCIL, PENCIL), PENCIL)
    k_s[at, :] = k_ref[...]
    v_s[at, :] = v_ref[...]

    @pl.when(i == 0)
    def _():
        pack_rows(q_ref, g_ref, out_ref, 0)

    @pl.when(i == PD // PENCIL - 1)
    def _():
        pack_rows(k_s, v_s, out_ref, HALF)


def pack(order, place, obj_query, grad_out, pattern_key, pattern_value):
    rows = pl.BlockSpec((PD, D), lambda i, order, place: (0, 0))
    block = pl.BlockSpec((PENCIL, D), lambda i, order, place: (order[place[0] + i] - place[1], 0))
    return pl.pallas_call(
        pack_kernel,
        out_shape=jax.ShapeDtypeStruct((H, PD, WIDE), BF16),
        grid_spec=pltpu.PrefetchScalarGridSpec(
            num_scalar_prefetch=2,
            grid=(PD // PENCIL,),
            in_specs=[rows, rows, block, block],
            out_specs=pl.BlockSpec((H, PD, WIDE), lambda i, order, place: (0, 0, 0)),
            scratch_shapes=[pltpu.VMEM((PD, D), BF16)] * 2,
        ),
        name="pack",
    )(order, place, obj_query, grad_out, pattern_key, pattern_value)


def unpack(ref, stores, turned=False):
    half = ROWS // 2
    for n, (start, width, offset) in enumerate(WINDOWS):
        out, base = stores[n % 2]
        if out is None:
            continue
        at = slice(base + n // 2 * half, base + n // 2 * half + half)
        x = ref[:, :, start : start + width].reshape(half, width)
        if turned:
            out[:, at] = mm(turned_shift(width, offset), x, CONTRACT_LAST)[: out.shape[0]].astype(BF16)
        else:
            out[at, :] = mm(x, shift(width, 128, offset, 0)).astype(BF16)


def stats_kernel(*refs):
    q_refs, kv_refs = refs[:N_Z], refs[N_Z : N_Z + 2]
    st_ref, q_s, g_s, k_s, v_s = refs[N_Z + 2 :]
    for n, ref in enumerate(kv_refs):
        unpack(ref, ((k_s, n * ROWS), (v_s, n * ROWS)))
    for n, ref in enumerate(q_refs):
        unpack(ref, ((q_s, n * ROWS), (g_s, n * ROWS)), turned=True)
    st_ref[...] = jnp.zeros_like(st_ref)

    for n in range(NQ // STQ):
        q0 = n * STQ
        qt = q_s[:, q0 : q0 + STQ]
        gt = g_s[:, q0 : q0 + STQ]

        def one_chunk(j, carry):
            m, l, w = carry
            k0 = pl.multiple_of(j * STK, STK)
            s = mm(k_s[pl.ds(k0, STK), :], qt).reshape(STK // SUB, SUB // 8, 8, STQ)
            d = mm(v_s[pl.ds(k0, STK), :], gt).reshape(STK // SUB, SUB // 8, 8, STQ)
            for i in range(STK // SUB):
                top = jnp.maximum(m, jnp.max(s[i], axis=0))
                fade = jnp.exp2((m - top) * C2)
                e = jnp.exp2((s[i] - top[None]) * C2)
                m, l, w = top, l * fade + jnp.sum(e, axis=0), w * fade + jnp.sum(e * d[i], axis=0)
            return m, l, w

        zero = jnp.zeros((8, STQ), F32)
        start = (jnp.full((8, STQ), NEG, F32), zero, zero)
        m, l, w = lax.fori_loop(0, NK // STK, one_chunk, start, unroll=SUN)
        top = jnp.max(m, axis=0, keepdims=True)
        fade = jnp.exp2((m - top) * C2)
        row, cols = q0 // (NQ // 2) * 4, slice(q0 % (NQ // 2), q0 % (NQ // 2) + STQ)
        st_ref[row : row + 1, cols] = top
        st_ref[row + 1 : row + 2, cols] = jnp.sum(l * fade, axis=0, keepdims=True)
        st_ref[row + 2 : row + 3, cols] = jnp.sum(w * fade, axis=0, keepdims=True)


def stats(queries, keys):
    return pl.pallas_call(
        stats_kernel,
        out_shape=jax.ShapeDtypeStruct((8, NQ // 2), F32),
        in_specs=[VMEM] * (N_Z + 2),
        out_specs=VMEM,
        scratch_shapes=[pltpu.VMEM((128, NQ), BF16)] * 2 + [pltpu.VMEM((NK, 128), BF16)] * 2,
        cost_estimate=pl.CostEstimate(flops=4 * NQ * NK * 256, transcendentals=NQ * NK, bytes_accessed=4 << 20),
        name="stats",
    )(*queries, *keys)


def block_of(ref, n):
    row, col = n // 2 * 4, n % 2 * ROWS
    return [ref[row + i : row + i + 1, col : col + ROWS] for i in range(3)]


def joined(parts):
    top = functools.reduce(jnp.maximum, [part[0] for part in parts])
    fades = [jnp.exp2((part[0] - top) * C2) for part in parts]
    total = sum(part[1] * fade for part, fade in zip(parts, fades))
    weighted = sum(part[2] * fade for part, fade in zip(parts, fades))
    return top * C2 + jnp.log2(total), weighted / total


def grads_kernel(*refs):
    q_refs, kv_refs, st_refs = refs[:N_Z], refs[N_Z : N_Z + 2], refs[N_Z + 2 : 2 * N_Z + 2]
    dkv_refs, dq_refs = refs[2 * N_Z + 2 : 2 * N_Z + 4], refs[2 * N_Z + 4 : 2 * N_Z + 6]
    scratch = refs[2 * N_Z + 6 :]
    q_s, g_s, k_s, v_s, t_s, dq_s, dk_s, dv_s, log_s, mean_s = scratch
    for n, ref in enumerate(kv_refs):
        unpack(ref, ((k_s, n * ROWS), (v_s, n * ROWS)))
        unpack(ref, ((t_s, n * ROWS), (None, 0)), turned=True)
    for n, ref in enumerate(q_refs):
        unpack(ref, ((q_s, n * ROWS), (g_s, n * ROWS)))
        log_now, mean_now = joined([block_of(st, n ^ t) for t, st in enumerate(st_refs)])
        here = slice(n * ROWS, (n + 1) * ROWS)
        log_s[:, here] = jnp.broadcast_to(log_now, (8, ROWS))
        mean_s[:, here] = jnp.broadcast_to(mean_now, (8, ROWS))
    dq_s[...] = jnp.zeros_like(dq_s)

    def one_chunk(j, _):
        k0 = pl.multiple_of(j * TK, TK)
        kc = k_s[pl.ds(k0, TK), :]
        vc = v_s[pl.ds(k0, TK), :]
        kt = t_s[:, pl.ds(k0, TK)]

        def one_tile(t, carry):
            dk, dv = carry
            q0 = pl.multiple_of(t * TQ, TQ)
            qt = q_s[pl.ds(q0, TQ), :]
            gt = g_s[pl.ds(q0, TQ), :]
            s = mm(kc, qt, CONTRACT_LAST).reshape(TK // 8, 8, TQ)
            d = mm(vc, gt, CONTRACT_LAST).reshape(TK // 8, 8, TQ)
            p = jnp.exp2(s * C2 - log_s[:, pl.ds(q0, TQ)][None])
            sg = ((d - mean_s[:, pl.ds(q0, TQ)][None]) * (p * SCALE)).astype(BF16).reshape(TK, TQ)
            p = p.astype(BF16).reshape(TK, TQ)
            dq_s[:, pl.ds(q0, TQ)] += mm(kt, sg)
            return dk + mm(sg, qt), dv + mm(p, gt)

        zero = jnp.zeros((TK, 128), F32)
        dk, dv = lax.fori_loop(0, NQ // TQ, one_tile, (zero, zero), unroll=GUN)
        dk_s[pl.ds(k0, TK), :] = dk.astype(BF16)
        dv_s[pl.ds(k0, TK), :] = dv.astype(BF16)
        return 0

    lax.fori_loop(0, NK // TK, one_chunk, 0)
    place4 = [shift(HD, cols, 0, dst) for _, cols, dst in WINDOWS]
    half = ROWS // 2
    for n, ref in enumerate(dkv_refs):
        base = n * ROWS
        parts = [
            mm((dk_s, dv_s)[i % 2][base + i // 2 * half : base + (i // 2 + 1) * half, :HD], place4[i]) for i in range(4)
        ]
        for k, piece in enumerate(pack_four(parts)):
            ref[:, :, k * 128 : (k + 1) * 128] = piece.reshape(N_G, HALF, 128)
    for n in range(N_Z):
        ref, row = dq_refs[n % 2], n // 2 * PENCIL
        parts = []
        for quarter in range(4):
            r0 = n * ROWS + quarter // 2 * half
            x = mm(dq_s[:, r0 : r0 + half].astype(BF16), place4[quarter], CONTRACT_FIRST)
            x = x.reshape(N_G, 2, PENCIL, x.shape[1])[:, quarter % 2]
            parts.append(x.reshape(N_G * PENCIL, x.shape[2]))
        for k, piece in enumerate(pack_four(parts)):
            ref[:, row : row + PENCIL, k * 128 : (k + 1) * 128] = piece.reshape(N_G, PENCIL, 128)


def grads(queries, keys, statistics):
    return pl.pallas_call(
        grads_kernel,
        out_shape=[jax.ShapeDtypeStruct((N_G, HALF, WIDE), BF16)] * 4,
        in_specs=[VMEM] * (2 * N_Z + 2),
        out_specs=[VMEM] * 4,
        scratch_shapes=[pltpu.VMEM((NQ, 128), BF16)] * 2
        + [pltpu.VMEM((NK, 128), BF16)] * 2
        + [pltpu.VMEM((HD, NK), BF16)]
        + [pltpu.VMEM((HD, NQ), F32)]
        + [pltpu.VMEM((NK, 128), BF16)] * 2
        + [pltpu.VMEM((8, NQ), F32)] * 2,
        cost_estimate=pl.CostEstimate(flops=10 * NQ * NK * 256, transcendentals=NQ * NK, bytes_accessed=8 << 20),
        name="grads",
    )(*queries, *keys, *statistics)


def meet_kernel(mine_ref, theirs_ref, keep_ref, send_ref):
    total = mine_ref[...].astype(F32) + theirs_ref[...].astype(F32)
    keep_ref[...] = total[:, :PENCIL]
    send_ref[...] = total[:, PENCIL:].astype(BF16)


def meet(mine, theirs):
    return pl.pallas_call(
        meet_kernel,
        out_shape=(
            jax.ShapeDtypeStruct((N_G, PENCIL, WIDE), F32),
            jax.ShapeDtypeStruct((N_G, PENCIL, WIDE), BF16),
        ),
        in_specs=[VMEM, VMEM],
        out_specs=(VMEM, VMEM),
        name="meet",
    )(mine, theirs)


def combine_kernel(*refs):
    out_ref = refs[-1]
    row = 0
    for parts in (refs[:2], refs[2:-1]):
        total = (parts[0][...].astype(F32) + parts[1][...].astype(F32)).astype(BF16)
        out_ref[:, row : row + total.shape[1], :] = total
        row += total.shape[1]


def combine(parts):
    return pl.pallas_call(
        combine_kernel,
        out_shape=jax.ShapeDtypeStruct((N_G, HALF + PENCIL, WIDE), BF16),
        in_specs=[VMEM] * len(parts),
        out_specs=VMEM,
        name="combine",
    )(*parts)


def finish_kernel(got_ref, query_ref, key_ref, value_ref):
    for h in range(H):
        here = slice(h * HD, (h + 1) * HD)
        for half in range(2):
            lane = half * 2 * HD
            rows = slice(half * HALF, (half + 1) * HALF)
            key_ref[rows, here] = got_ref[h, :HALF, lane : lane + HD]
            value_ref[rows, here] = got_ref[h, :HALF, lane + HD : lane + 2 * HD]
        for quarter in range(4):
            rows = slice(quarter * PENCIL, (quarter + 1) * PENCIL)
            query_ref[rows, here] = got_ref[h, HALF:, quarter * HD : (quarter + 1) * HD]


def finish(got):
    return pl.pallas_call(
        finish_kernel,
        out_shape=[jax.ShapeDtypeStruct((PD, D), BF16)] * 3,
        in_specs=[VMEM],
        out_specs=[VMEM] * 3,
        name="finish",
    )(got)


def over_a(x):
    return lax.ppermute(x, Z, ((0, 3), (3, 0), (1, 2), (2, 1)))


def over_b(x):
    return lax.ppermute(x, Z, ((0, 1), (1, 0), (2, 3), (3, 2)))


def over_core(x):
    return lax.ppermute(x, CORE, ((0, 1), (1, 0)))


def to_heads(x):
    return lax.all_to_all(x, HEADS, 0, 0, tiled=True)


def layer(obj_query, grad_out, pattern_key, pattern_value, pencil_order):
    place = jnp.stack(
        [lax.axis_index(BLK_GRP) * (PD // PENCIL), lax.axis_index(GRP) * (pattern_key.shape[0] // PENCIL)]
    ).astype(jnp.int32)
    sent = pack(pencil_order, place, obj_query, grad_out, pattern_key, pattern_value)
    got = to_heads(sent)
    queries, keys = [got[:, :HALF]], [got[:, HALF:]]
    third = over_b(queries[0])
    keys.append(over_a(keys[0]))
    queries += [over_core(queries[0]), third, over_core(third)]
    statistics = [stats(queries, keys)]
    third = over_b(statistics[0])
    statistics += [over_core(statistics[0]), third, over_core(third)]
    keys_here, keys_there, queries_here, queries_there = grads(queries, keys, statistics)
    keys_got = over_a(keys_there)
    queries_got = over_core(queries_there)
    keep, send = meet(queries_here, queries_got)
    queries_got = over_b(send)
    total = combine([keys_here, keys_got, keep, queries_got])
    total = to_heads(total)
    return tuple(finish(total))


def solution(mesh):
    split = Mesh(mesh.devices.reshape(4, 2, 2, 4, 2), BLK_GRP)
    return jax.shard_map(
        layer,
        mesh=split,
        in_specs=(P(BLK_GRP, None), P(BLK_GRP, None), P(GRP, None), P(GRP, None), P()),
        out_specs=(P(BLK_GRP, None), P(BLK_GRP, None), P(BLK_GRP, None)),
        check_vma=False,
    )
```

```python
import functools
import math

import jax
import jax.numpy as jnp
from jax import lax
from jax.experimental import pallas as pl
from jax.experimental.pallas import tpu as pltpu
from jax.sharding import Mesh
from jax.sharding import PartitionSpec as P


D = 1536
H = 16
HD = D // H
PENCIL = 16
PD = 64
HALF = PD // 2
WIDE = 4 * HD
N_Z = 4
N_G = 16
BLK_GRP = ("blk_0", "blk_1", "grp_0", "grp_1", "grp_2")
GRP = ("grp_0", "grp_1", "grp_2")
HEADS = ("blk_1", "grp_0", "grp_1")
Z = "blk_0"
CORE = "grp_2"
SCALE = 1.0 / math.sqrt(HD)
C2 = SCALE * math.log2(math.e)
TQ = 1024
TK = 512
GUN = 4
SUB = 64
NEG = -1e30
F32 = jnp.float32
BF16 = jnp.bfloat16
CONTRACT_LAST = (((1,), (1,)), ((), ()))
CONTRACT_FIRST = (((0,), (0,)), ((), ()))
ROWS = N_G * PD
NQ = N_Z * ROWS
NK = 2 * ROWS
VMEM = pl.BlockSpec(memory_space=pltpu.VMEM)

WINDOWS = ((0, 128, 0), (0, 256, HD), (128, 256, 2 * HD - 128), (256, 128, 3 * HD - 256))


def mm(a, b, dims=(((1,), (0,)), ((), ()))):
    return lax.dot_general(a, b, dims, preferred_element_type=F32)


def shift(rows, cols, src, dst):
    i = lax.broadcasted_iota(jnp.int32, (rows, cols), 0) - src
    j = lax.broadcasted_iota(jnp.int32, (rows, cols), 1) - dst
    return jnp.where((i == j) & (i >= 0) & (i < HD), 1.0, 0.0).astype(BF16)


def turned_shift(cols, src):
    i = lax.broadcasted_iota(jnp.int32, (128, cols), 0)
    j = lax.broadcasted_iota(jnp.int32, (128, cols), 1) - src
    return jnp.where((i == j) & (i < HD), 1.0, 0.0).astype(BF16)


def pack_four(parts):
    a, b, c, d = parts
    return (
        (a + b[:, :128]).astype(BF16),
        (b[:, 128:] + c[:, :128]).astype(BF16),
        (c[:, 128:] + d).astype(BF16),
    )


def pack_kernel(order_ref, place_ref, q_ref, g_ref, k_ref, v_ref, out_ref, a_s, b_s):
    i = pl.program_id(0)
    at = pl.ds(pl.multiple_of(i // 2 * PD + HALF + i % 2 * PENCIL, PENCIL), PENCIL)
    a_s[at, :] = k_ref[...]
    b_s[at, :] = v_ref[...]

    @pl.when(i == PD // PENCIL - 1)
    def _():
        for half in range(2):
            rows = slice(half * HALF, (half + 1) * HALF)
            a_s[half * PD : half * PD + HALF, :] = q_ref[rows, :]
            b_s[half * PD : half * PD + HALF, :] = g_ref[rows, :]
        for turn in range(4):
            heads = range(turn, H, 4)
            offset = turn * HD % 128
            width = 128 if offset + HD <= 128 else 256
            parts = []
            for n, (_, cols, dst) in enumerate(WINDOWS):
                ref = (a_s, b_s)[n % 2]
                rows = slice(n // 2 * PD, (n // 2 + 1) * PD)
                x = [ref[rows, h * HD // 128 * 128 : h * HD // 128 * 128 + width] for h in heads]
                parts.append(mm(jnp.concatenate(x, axis=0), shift(width, cols, offset, dst)))
            for n, piece in enumerate(pack_four(parts)):
                for k, h in enumerate(heads):
                    out_ref[h, :, n * 128 : (n + 1) * 128] = piece[k * PD : (k + 1) * PD]


def pack(order, place, obj_query, grad_out, pattern_key, pattern_value):
    rows = pl.BlockSpec((PD, D), lambda i, order, place: (0, 0))
    block = pl.BlockSpec((PENCIL, D), lambda i, order, place: (order[place[0] + i] - place[1], 0))
    return pl.pallas_call(
        pack_kernel,
        out_shape=jax.ShapeDtypeStruct((H, PD, WIDE), BF16),
        grid_spec=pltpu.PrefetchScalarGridSpec(
            num_scalar_prefetch=2,
            grid=(PD // PENCIL,),
            in_specs=[rows, rows, block, block],
            out_specs=pl.BlockSpec((H, PD, WIDE), lambda i, order, place: (0, 0, 0)),
            scratch_shapes=[pltpu.VMEM((2 * PD, D), BF16)] * 2,
        ),
        name="pack",
    )(order, place, obj_query, grad_out, pattern_key, pattern_value)


def unpack(ref, stores, turned=False):
    half = ROWS // 2
    for n, (start, width, offset) in enumerate(WINDOWS):
        out, base = stores[n % 2]
        if out is None:
            continue
        at = slice(base + n // 2 * half, base + n // 2 * half + half)
        x = ref[:, :, start : start + width].reshape(half, width)
        if turned:
            out[:, at] = mm(turned_shift(width, offset), x, CONTRACT_LAST)[: out.shape[0]].astype(BF16)
        else:
            out[at, :] = mm(x, shift(width, 128, offset, 0)).astype(BF16)


def sweep(state, k_ref, v_ref, qt, gt):
    m, l, w = state
    rows, cols = k_ref.shape[0], qt.shape[1]
    s = mm(k_ref[...], qt).reshape(rows // SUB, SUB // 8, 8, cols)
    d = mm(v_ref[...], gt).reshape(rows // SUB, SUB // 8, 8, cols)
    for i in range(rows // SUB):
        top = jnp.maximum(m, jnp.max(s[i], axis=0))
        fade = jnp.exp2((m - top) * C2)
        e = jnp.exp2((s[i] - top[None]) * C2)
        m, l, w = top, l * fade + jnp.sum(e, axis=0), w * fade + jnp.sum(e * d[i], axis=0)
    return m, l, w


def write_stats(st_ref, n, state):
    m, l, w = state
    top = jnp.max(m, axis=0, keepdims=True)
    fade = jnp.exp2((m - top) * C2)
    row, cols = n // 2 * 4, slice(n % 2 * ROWS, (n % 2 + 1) * ROWS)
    st_ref[row : row + 1, cols] = top
    st_ref[row + 1 : row + 2, cols] = jnp.sum(l * fade, axis=0, keepdims=True)
    st_ref[row + 2 : row + 3, cols] = jnp.sum(w * fade, axis=0, keepdims=True)


def first_stats_kernel(qa_ref, qb_ref, kv_ref, st_ref, q_ref, g_ref, k_ref, v_ref):
    unpack(kv_ref, ((k_ref, 0), (v_ref, 0)))
    for n, ref in enumerate((qa_ref, qb_ref)):
        unpack(ref, ((q_ref, n * ROWS), (g_ref, n * ROWS)), turned=True)
    st_ref[...] = jnp.zeros_like(st_ref)
    for n in range(2):
        here = slice(n * ROWS, (n + 1) * ROWS)
        zero = jnp.zeros((8, ROWS), F32)
        state = (jnp.full((8, ROWS), NEG, F32), zero, zero)
        write_stats(st_ref, n, sweep(state, k_ref, v_ref, q_ref[:, here], g_ref[:, here]))


def first_stats(qa, qb, kv):
    return pl.pallas_call(
        first_stats_kernel,
        out_shape=[jax.ShapeDtypeStruct((8, NQ // 2), F32)]
        + [jax.ShapeDtypeStruct((128, 2 * ROWS), BF16)] * 2
        + [jax.ShapeDtypeStruct((ROWS, 128), BF16)] * 2,
        in_specs=[VMEM] * 3,
        out_specs=[VMEM] * 5,
        cost_estimate=pl.CostEstimate(flops=NQ * NK * 256, transcendentals=NQ * NK // 4, bytes_accessed=2 << 20),
        name="first_stats",
    )(qa, qb, kv)


def stats_kernel(
    qa_ref, qb_ref, kv_ref, part_ref, q_own, g_own, k_own, v_own, st_ref, q_s, g_s, k_s, v_s
):
    unpack(kv_ref, ((k_s, 0), (v_s, 0)))
    for n, ref in enumerate((qa_ref, qb_ref)):
        unpack(ref, ((q_s, n * ROWS), (g_s, n * ROWS)), turned=True)
    st_ref[...] = jnp.zeros_like(st_ref)
    zero = jnp.zeros((8, ROWS), F32)
    for n in range(2):
        here = slice(n * ROWS, (n + 1) * ROWS)
        top, total, weighted = (part_ref[i : i + 1, here] for i in range(3))
        first = lax.broadcasted_iota(jnp.int32, (8, ROWS), 0) == 0
        state = (zero + top, jnp.where(first, total, zero), jnp.where(first, weighted, zero))
        write_stats(st_ref, n, sweep(state, k_s, v_s, q_own[:, here], g_own[:, here]))
    for n in range(2):
        here = slice(n * ROWS, (n + 1) * ROWS)
        qt, gt = q_s[:, here], g_s[:, here]
        state = sweep((jnp.full((8, ROWS), NEG, F32), zero, zero), k_own, v_own, qt, gt)
        write_stats(st_ref, 2 + n, sweep(state, k_s, v_s, qt, gt))


def stats(qa, qb, kv, first):
    return pl.pallas_call(
        stats_kernel,
        out_shape=jax.ShapeDtypeStruct((8, NQ // 2), F32),
        in_specs=[VMEM] * 8,
        out_specs=VMEM,
        scratch_shapes=[pltpu.VMEM((128, 2 * ROWS), BF16)] * 2 + [pltpu.VMEM((ROWS, 128), BF16)] * 2,
        cost_estimate=pl.CostEstimate(flops=3 * NQ * NK * 256, transcendentals=NQ * NK, bytes_accessed=4 << 20),
        name="stats",
    )(qa, qb, kv, *first)


def rows_kernel(*refs):
    q_refs, kv_refs = refs[:N_Z], refs[N_Z : N_Z + 2]
    q_s, g_s, k_s, v_s, t_s = refs[N_Z + 2 :]
    for n, ref in enumerate(kv_refs):
        unpack(ref, ((k_s, n * ROWS), (v_s, n * ROWS)))
        unpack(ref, ((t_s, n * ROWS), (None, 0)), turned=True)
    for n, ref in enumerate(q_refs):
        unpack(ref, ((q_s, n * ROWS), (g_s, n * ROWS)))


def rows_of(queries, keys):
    return pl.pallas_call(
        rows_kernel,
        out_shape=[jax.ShapeDtypeStruct((NQ, 128), BF16)] * 2
        + [jax.ShapeDtypeStruct((NK, 128), BF16)] * 2
        + [jax.ShapeDtypeStruct((HD, NK), BF16)],
        in_specs=[VMEM] * (N_Z + 2),
        out_specs=[VMEM] * 5,
        name="rows_of",
    )(*queries, *keys)


def block_of(ref, n):
    row, col = n // 2 * 4, n % 2 * ROWS
    return [ref[row + i : row + i + 1, col : col + ROWS] for i in range(3)]


def joined(parts):
    top = functools.reduce(jnp.maximum, [part[0] for part in parts])
    fades = [jnp.exp2((part[0] - top) * C2) for part in parts]
    total = sum(part[1] * fade for part, fade in zip(parts, fades))
    weighted = sum(part[2] * fade for part, fade in zip(parts, fades))
    return top * C2 + jnp.log2(total), weighted / total


def grads_kernel(*refs):
    q_s, g_s, k_s, v_s, t_s = refs[:5]
    st_refs, dkv_refs, dq_refs = refs[5 : 5 + N_Z], refs[5 + N_Z : 7 + N_Z], refs[7 + N_Z : 9 + N_Z]
    dq_s, dk_s, dv_s, log_s, mean_s = refs[9 + N_Z :]
    for n in range(N_Z):
        log_now, mean_now = joined([block_of(st, n ^ t) for t, st in enumerate(st_refs)])
        here = slice(n * ROWS, (n + 1) * ROWS)
        log_s[:, here] = jnp.broadcast_to(log_now, (8, ROWS))
        mean_s[:, here] = jnp.broadcast_to(mean_now, (8, ROWS))
    dq_s[...] = jnp.zeros_like(dq_s)

    def one_chunk(j, _):
        k0 = pl.multiple_of(j * TK, TK)
        kc = k_s[pl.ds(k0, TK), :]
        vc = v_s[pl.ds(k0, TK), :]
        kt = t_s[:, pl.ds(k0, TK)]

        def one_tile(t, carry):
            dk, dv = carry
            q0 = pl.multiple_of(t * TQ, TQ)
            qt = q_s[pl.ds(q0, TQ), :]
            gt = g_s[pl.ds(q0, TQ), :]
            s = mm(kc, qt, CONTRACT_LAST).reshape(TK // 8, 8, TQ)
            d = mm(vc, gt, CONTRACT_LAST).reshape(TK // 8, 8, TQ)
            p = jnp.exp2(s * C2 - log_s[:, pl.ds(q0, TQ)][None])
            sg = ((d - mean_s[:, pl.ds(q0, TQ)][None]) * (p * SCALE)).astype(BF16).reshape(TK, TQ)
            p = p.astype(BF16).reshape(TK, TQ)
            dq_s[:, pl.ds(q0, TQ)] += mm(kt, sg)
            return dk + mm(sg, qt), dv + mm(p, gt)

        zero = jnp.zeros((TK, 128), F32)
        dk, dv = lax.fori_loop(0, NQ // TQ, one_tile, (zero, zero), unroll=GUN)
        dk_s[pl.ds(k0, TK), :] = dk.astype(BF16)
        dv_s[pl.ds(k0, TK), :] = dv.astype(BF16)
        return 0

    lax.fori_loop(0, NK // TK, one_chunk, 0)
    place4 = [shift(HD, cols, 0, dst) for _, cols, dst in WINDOWS]
    half = ROWS // 2
    for n, ref in enumerate(dkv_refs):
        base = n * ROWS
        parts = [
            mm((dk_s, dv_s)[i % 2][base + i // 2 * half : base + (i // 2 + 1) * half, :HD], place4[i]) for i in range(4)
        ]
        for k, piece in enumerate(pack_four(parts)):
            ref[:, :, k * 128 : (k + 1) * 128] = piece.reshape(N_G, HALF, 128)
    for n in range(N_Z):
        ref, row = dq_refs[n % 2], n // 2 * PENCIL
        parts = []
        for quarter in range(4):
            r0 = n * ROWS + quarter // 2 * half
            x = mm(dq_s[:, r0 : r0 + half].astype(BF16), place4[quarter], CONTRACT_FIRST)
            x = x.reshape(N_G, 2, PENCIL, x.shape[1])[:, quarter % 2]
            parts.append(x.reshape(N_G * PENCIL, x.shape[2]))
        for k, piece in enumerate(pack_four(parts)):
            ref[:, row : row + PENCIL, k * 128 : (k + 1) * 128] = piece.reshape(N_G, PENCIL, 128)


def grads(rows, statistics):
    return pl.pallas_call(
        grads_kernel,
        out_shape=[jax.ShapeDtypeStruct((N_G, HALF, WIDE), BF16)] * 4,
        in_specs=[VMEM] * (5 + N_Z),
        out_specs=[VMEM] * 4,
        scratch_shapes=[pltpu.VMEM((HD, NQ), F32)]
        + [pltpu.VMEM((NK, 128), BF16)] * 2
        + [pltpu.VMEM((8, NQ), F32)] * 2,
        cost_estimate=pl.CostEstimate(flops=10 * NQ * NK * 256, transcendentals=NQ * NK, bytes_accessed=8 << 20),
        name="grads",
    )(*rows, *statistics)


def meet_kernel(mine_ref, theirs_ref, keep_ref, send_ref):
    total = mine_ref[...].astype(F32) + theirs_ref[...].astype(F32)
    keep_ref[...] = total[:, :PENCIL]
    send_ref[...] = total[:, PENCIL:].astype(BF16)


def meet(mine, theirs):
    return pl.pallas_call(
        meet_kernel,
        out_shape=(
            jax.ShapeDtypeStruct((N_G, PENCIL, WIDE), F32),
            jax.ShapeDtypeStruct((N_G, PENCIL, WIDE), BF16),
        ),
        in_specs=[VMEM, VMEM],
        out_specs=(VMEM, VMEM),
        name="meet",
    )(mine, theirs)


def combine_kernel(*refs):
    out_ref = refs[-1]
    row = 0
    for parts in (refs[:2], refs[2:-1]):
        total = (parts[0][...].astype(F32) + parts[1][...].astype(F32)).astype(BF16)
        out_ref[:, row : row + total.shape[1], :] = total
        row += total.shape[1]


def combine(parts):
    return pl.pallas_call(
        combine_kernel,
        out_shape=jax.ShapeDtypeStruct((N_G, HALF + PENCIL, WIDE), BF16),
        in_specs=[VMEM] * len(parts),
        out_specs=VMEM,
        name="combine",
    )(*parts)


def finish_kernel(got_ref, query_ref, key_ref, value_ref):
    for h in range(H):
        here = slice(h * HD, (h + 1) * HD)
        for half in range(2):
            lane = half * 2 * HD
            rows = slice(half * HALF, (half + 1) * HALF)
            key_ref[rows, here] = got_ref[h, :HALF, lane : lane + HD]
            value_ref[rows, here] = got_ref[h, :HALF, lane + HD : lane + 2 * HD]
        for quarter in range(4):
            rows = slice(quarter * PENCIL, (quarter + 1) * PENCIL)
            query_ref[rows, here] = got_ref[h, HALF:, quarter * HD : (quarter + 1) * HD]


def finish(got):
    return pl.pallas_call(
        finish_kernel,
        out_shape=[jax.ShapeDtypeStruct((PD, D), BF16)] * 3,
        in_specs=[VMEM],
        out_specs=[VMEM] * 3,
        name="finish",
    )(got)


def over_a(x):
    return lax.ppermute(x, Z, ((0, 3), (3, 0), (1, 2), (2, 1)))


def over_b(x):
    return lax.ppermute(x, Z, ((0, 1), (1, 0), (2, 3), (3, 2)))


def over_core(x):
    return lax.ppermute(x, CORE, ((0, 1), (1, 0)))


def to_heads(x):
    return lax.all_to_all(x, HEADS, 0, 0, tiled=True)


def layer(obj_query, grad_out, pattern_key, pattern_value, pencil_order):
    place = jnp.stack(
        [lax.axis_index(BLK_GRP) * (PD // PENCIL), lax.axis_index(GRP) * (pattern_key.shape[0] // PENCIL)]
    ).astype(jnp.int32)
    sent = pack(pencil_order, place, obj_query, grad_out, pattern_key, pattern_value)
    got = to_heads(sent)
    queries, keys = [got[:, :HALF]], [got[:, HALF:]]
    queries.append(over_core(queries[0]))
    queries.append(over_b(queries[0]))
    keys.append(over_a(keys[0]))
    first = first_stats(queries[0], queries[1], keys[0])
    queries.append(over_core(queries[2]))
    statistics = [stats(queries[2], queries[3], keys[1], first)]
    third = over_b(statistics[0])
    statistics += [over_core(statistics[0]), third, over_core(third)]
    rows = rows_of(queries, keys)
    keys_here, keys_there, queries_here, queries_there = grads(rows, statistics)
    keys_got = over_a(keys_there)
    queries_got = over_core(queries_there)
    keep, send = meet(queries_here, queries_got)
    queries_got = over_b(send)
    total = combine([keys_here, keys_got, keep, queries_got])
    total = to_heads(total)
    return tuple(finish(total))


def solution(mesh):
    split = Mesh(mesh.devices.reshape(4, 2, 2, 4, 2), BLK_GRP)
    return jax.shard_map(
        layer,
        mesh=split,
        in_specs=(P(BLK_GRP, None), P(BLK_GRP, None), P(GRP, None), P(GRP, None), P()),
        out_specs=(P(BLK_GRP, None), P(BLK_GRP, None), P(BLK_GRP, None)),
        check_vma=False,
    )
```

```python
import functools
import math

import jax
import jax.numpy as jnp
from jax import lax
from jax.experimental import pallas as pl
from jax.experimental.pallas import tpu as pltpu
from jax.sharding import Mesh
from jax.sharding import PartitionSpec as P


D = 1536
H = 16
HD = D // H
PENCIL = 16
PD = 64
HALF = PD // 2
WIDE = 4 * HD
N_Z = 4
N_G = 16
BLK_GRP = ("blk_0", "blk_1", "grp_0", "grp_1", "grp_2")
GRP = ("grp_0", "grp_1", "grp_2")
HEADS = ("blk_1", "grp_0", "grp_1")
Z = "blk_0"
CORE = "grp_2"
SCALE = 1.0 / math.sqrt(HD)
C2 = SCALE * math.log2(math.e)
TQ = 1024
TK = 512
GUN = 4
SUB = 64
NEG = -1e30
F32 = jnp.float32
BF16 = jnp.bfloat16
CONTRACT_LAST = (((1,), (1,)), ((), ()))
CONTRACT_FIRST = (((0,), (0,)), ((), ()))
ROWS = N_G * PD
NQ = N_Z * ROWS
NK = 2 * ROWS
VMEM = pl.BlockSpec(memory_space=pltpu.VMEM)


def here(*arrays):
    return [pltpu.with_memory_space_constraint(x, pltpu.VMEM) for x in arrays]


def away(x):
    return pltpu.with_memory_space_constraint(x, pltpu.HBM)


WINDOWS = ((0, 128, 0), (0, 256, HD), (128, 256, 2 * HD - 128), (256, 128, 3 * HD - 256))


def mm(a, b, dims=(((1,), (0,)), ((), ()))):
    return lax.dot_general(a, b, dims, preferred_element_type=F32)


def shift(rows, cols, src, dst):
    i = lax.broadcasted_iota(jnp.int32, (rows, cols), 0) - src
    j = lax.broadcasted_iota(jnp.int32, (rows, cols), 1) - dst
    return jnp.where((i == j) & (i >= 0) & (i < HD), 1.0, 0.0).astype(BF16)


def turned_shift(cols, src):
    i = lax.broadcasted_iota(jnp.int32, (128, cols), 0)
    j = lax.broadcasted_iota(jnp.int32, (128, cols), 1) - src
    return jnp.where((i == j) & (i < HD), 1.0, 0.0).astype(BF16)


def pack_four(parts):
    a, b, c, d = parts
    return (
        (a + b[:, :128]).astype(BF16),
        (b[:, 128:] + c[:, :128]).astype(BF16),
        (c[:, 128:] + d).astype(BF16),
    )


def pack_kernel(order_ref, place_ref, q_ref, g_ref, k_ref, v_ref, out_ref, a_s, b_s):
    i = pl.program_id(0)
    at = pl.ds(pl.multiple_of(i // 2 * PD + HALF + i % 2 * PENCIL, PENCIL), PENCIL)
    a_s[at, :] = k_ref[...]
    b_s[at, :] = v_ref[...]

    @pl.when(i == PD // PENCIL - 1)
    def _():
        for half in range(2):
            rows = slice(half * HALF, (half + 1) * HALF)
            a_s[half * PD : half * PD + HALF, :] = q_ref[rows, :]
            b_s[half * PD : half * PD + HALF, :] = g_ref[rows, :]
        for turn in range(4):
            heads = range(turn, H, 4)
            offset = turn * HD % 128
            width = 128 if offset + HD <= 128 else 256
            parts = []
            for n, (_, cols, dst) in enumerate(WINDOWS):
                ref = (a_s, b_s)[n % 2]
                rows = slice(n // 2 * PD, (n // 2 + 1) * PD)
                x = [ref[rows, h * HD // 128 * 128 : h * HD // 128 * 128 + width] for h in heads]
                parts.append(mm(jnp.concatenate(x, axis=0), shift(width, cols, offset, dst)))
            for n, piece in enumerate(pack_four(parts)):
                for k, h in enumerate(heads):
                    out_ref[h, :, n * 128 : (n + 1) * 128] = piece[k * PD : (k + 1) * PD]


def pack(order, place, obj_query, grad_out, pattern_key, pattern_value):
    rows = pl.BlockSpec((PD, D), lambda i, order, place: (0, 0))
    block = pl.BlockSpec((PENCIL, D), lambda i, order, place: (order[place[0] + i] - place[1], 0))
    return pl.pallas_call(
        pack_kernel,
        out_shape=jax.ShapeDtypeStruct((H, PD, WIDE), BF16),
        grid_spec=pltpu.PrefetchScalarGridSpec(
            num_scalar_prefetch=2,
            grid=(PD // PENCIL,),
            in_specs=[rows, rows, block, block],
            out_specs=pl.BlockSpec((H, PD, WIDE), lambda i, order, place: (0, 0, 0)),
            scratch_shapes=[pltpu.VMEM((2 * PD, D), BF16)] * 2,
        ),
        compiler_params=pltpu.CompilerParams(vmem_limit_bytes=16 << 20),
        name="pack",
    )(away(order), place, *map(away, (obj_query, grad_out, pattern_key, pattern_value)))


def unpack(ref, stores, turned=False):
    half = ROWS // 2
    for n, (start, width, offset) in enumerate(WINDOWS):
        out, base = stores[n % 2]
        if out is None:
            continue
        at = slice(base + n // 2 * half, base + n // 2 * half + half)
        x = ref[:, :, start : start + width].reshape(half, width)
        if turned:
            out[:, at] = mm(turned_shift(width, offset), x, CONTRACT_LAST)[: out.shape[0]].astype(BF16)
        else:
            out[at, :] = mm(x, shift(width, 128, offset, 0)).astype(BF16)


def sweep(state, k_ref, v_ref, qt, gt):
    m, l, w = state
    rows, cols = k_ref.shape[0], qt.shape[1]
    s = mm(k_ref[...], qt).reshape(rows // SUB, SUB // 8, 8, cols)
    d = mm(v_ref[...], gt).reshape(rows // SUB, SUB // 8, 8, cols)
    for i in range(rows // SUB):
        top = jnp.maximum(m, jnp.max(s[i], axis=0))
        fade = jnp.exp2((m - top) * C2)
        e = jnp.exp2((s[i] - top[None]) * C2)
        m, l, w = top, l * fade + jnp.sum(e, axis=0), w * fade + jnp.sum(e * d[i], axis=0)
    return m, l, w


def write_stats(st_ref, n, state):
    m, l, w = state
    top = jnp.max(m, axis=0, keepdims=True)
    fade = jnp.exp2((m - top) * C2)
    row, cols = n // 2 * 4, slice(n % 2 * ROWS, (n % 2 + 1) * ROWS)
    st_ref[row : row + 1, cols] = top
    st_ref[row + 1 : row + 2, cols] = jnp.sum(l * fade, axis=0, keepdims=True)
    st_ref[row + 2 : row + 3, cols] = jnp.sum(w * fade, axis=0, keepdims=True)


def first_stats_kernel(qa_ref, qb_ref, kv_ref, st_ref, q_ref, g_ref, k_ref, v_ref):
    unpack(kv_ref, ((k_ref, 0), (v_ref, 0)))
    for n, ref in enumerate((qa_ref, qb_ref)):
        unpack(ref, ((q_ref, n * ROWS), (g_ref, n * ROWS)), turned=True)
    st_ref[...] = jnp.zeros_like(st_ref)
    for n in range(2):
        here = slice(n * ROWS, (n + 1) * ROWS)
        zero = jnp.zeros((8, ROWS), F32)
        state = (jnp.full((8, ROWS), NEG, F32), zero, zero)
        write_stats(st_ref, n, sweep(state, k_ref, v_ref, q_ref[:, here], g_ref[:, here]))


def first_stats(qa, qb, kv):
    return pl.pallas_call(
        first_stats_kernel,
        out_shape=[pltpu.VMEM((8, NQ // 2), F32)]
        + [pltpu.VMEM((128, 2 * ROWS), BF16)] * 2
        + [pltpu.VMEM((ROWS, 128), BF16)] * 2,
        in_specs=[VMEM] * 3,
        out_specs=[VMEM] * 5,
        cost_estimate=pl.CostEstimate(flops=NQ * NK * 256, transcendentals=NQ * NK // 4, bytes_accessed=2 << 20),
        compiler_params=pltpu.CompilerParams(vmem_limit_bytes=32 << 20),
        name="first_stats",
    )(*here(qa, qb, kv))


def stats_kernel(
    qa_ref, qb_ref, kv_ref, part_ref, q_own, g_own, k_own, v_own, st_ref, q_s, g_s, k_s, v_s
):
    unpack(kv_ref, ((k_s, 0), (v_s, 0)))
    for n, ref in enumerate((qa_ref, qb_ref)):
        unpack(ref, ((q_s, n * ROWS), (g_s, n * ROWS)), turned=True)
    st_ref[...] = jnp.zeros_like(st_ref)
    zero = jnp.zeros((8, ROWS), F32)
    for n in range(2):
        here = slice(n * ROWS, (n + 1) * ROWS)
        top, total, weighted = (part_ref[i : i + 1, here] for i in range(3))
        first = lax.broadcasted_iota(jnp.int32, (8, ROWS), 0) == 0
        state = (zero + top, jnp.where(first, total, zero), jnp.where(first, weighted, zero))
        write_stats(st_ref, n, sweep(state, k_s, v_s, q_own[:, here], g_own[:, here]))
    for n in range(2):
        here = slice(n * ROWS, (n + 1) * ROWS)
        qt, gt = q_s[:, here], g_s[:, here]
        state = sweep((jnp.full((8, ROWS), NEG, F32), zero, zero), k_own, v_own, qt, gt)
        write_stats(st_ref, 2 + n, sweep(state, k_s, v_s, qt, gt))


def stats(qa, qb, kv, first):
    return pl.pallas_call(
        stats_kernel,
        out_shape=pltpu.VMEM((8, NQ // 2), F32),
        in_specs=[VMEM] * 8,
        out_specs=VMEM,
        scratch_shapes=[pltpu.VMEM((128, 2 * ROWS), BF16)] * 2 + [pltpu.VMEM((ROWS, 128), BF16)] * 2,
        cost_estimate=pl.CostEstimate(flops=3 * NQ * NK * 256, transcendentals=NQ * NK, bytes_accessed=4 << 20),
        compiler_params=pltpu.CompilerParams(vmem_limit_bytes=36 << 20),
        name="stats",
    )(*here(qa, qb, kv, *first))


def rows_kernel(*refs):
    q_refs, kv_refs = refs[:N_Z], refs[N_Z : N_Z + 2]
    q_s, g_s, k_s, v_s, t_s = refs[N_Z + 2 :]
    for n, ref in enumerate(kv_refs):
        unpack(ref, ((k_s, n * ROWS), (v_s, n * ROWS)))
        unpack(ref, ((t_s, n * ROWS), (None, 0)), turned=True)
    for n, ref in enumerate(q_refs):
        unpack(ref, ((q_s, n * ROWS), (g_s, n * ROWS)))


def rows_of(queries, keys):
    return pl.pallas_call(
        rows_kernel,
        out_shape=[pltpu.VMEM((NQ, 128), BF16)] * 2
        + [pltpu.VMEM((NK, 128), BF16)] * 2
        + [pltpu.VMEM((HD, NK), BF16)],
        in_specs=[VMEM] * (N_Z + 2),
        out_specs=[VMEM] * 5,
        compiler_params=pltpu.CompilerParams(vmem_limit_bytes=24 << 20),
        name="rows_of",
    )(*here(*queries, *keys))


def block_of(ref, n):
    row, col = n // 2 * 4, n % 2 * ROWS
    return [ref[row + i : row + i + 1, col : col + ROWS] for i in range(3)]


def joined(parts):
    top = functools.reduce(jnp.maximum, [part[0] for part in parts])
    fades = [jnp.exp2((part[0] - top) * C2) for part in parts]
    total = sum(part[1] * fade for part, fade in zip(parts, fades))
    weighted = sum(part[2] * fade for part, fade in zip(parts, fades))
    return top * C2 + jnp.log2(total), weighted / total


def grads_kernel(*refs):
    q_s, g_s, k_s, v_s, t_s = refs[:5]
    st_refs, dkv_refs, dq_refs = refs[5 : 5 + N_Z], refs[5 + N_Z : 7 + N_Z], refs[7 + N_Z : 9 + N_Z]
    dq_s, dk_s, dv_s, log_s, mean_s = refs[9 + N_Z :]
    for n in range(N_Z):
        log_now, mean_now = joined([block_of(st, n ^ t) for t, st in enumerate(st_refs)])
        here = slice(n * ROWS, (n + 1) * ROWS)
        log_s[:, here] = jnp.broadcast_to(log_now, (8, ROWS))
        mean_s[:, here] = jnp.broadcast_to(mean_now, (8, ROWS))
    dq_s[...] = jnp.zeros_like(dq_s)

    def one_chunk(j, _):
        k0 = pl.multiple_of(j * TK, TK)
        kc = k_s[pl.ds(k0, TK), :]
        vc = v_s[pl.ds(k0, TK), :]
        kt = t_s[:, pl.ds(k0, TK)]

        def one_tile(t, carry):
            dk, dv = carry
            q0 = pl.multiple_of(t * TQ, TQ)
            qt = q_s[pl.ds(q0, TQ), :]
            gt = g_s[pl.ds(q0, TQ), :]
            s = mm(kc, qt, CONTRACT_LAST).reshape(TK // 8, 8, TQ)
            d = mm(vc, gt, CONTRACT_LAST).reshape(TK // 8, 8, TQ)
            p = jnp.exp2(s * C2 - log_s[:, pl.ds(q0, TQ)][None])
            sg = ((d - mean_s[:, pl.ds(q0, TQ)][None]) * (p * SCALE)).astype(BF16).reshape(TK, TQ)
            p = p.astype(BF16).reshape(TK, TQ)
            dq_s[:, pl.ds(q0, TQ)] += mm(kt, sg)
            return dk + mm(sg, qt), dv + mm(p, gt)

        zero = jnp.zeros((TK, 128), F32)
        dk, dv = lax.fori_loop(0, NQ // TQ, one_tile, (zero, zero), unroll=GUN)
        dk_s[pl.ds(k0, TK), :] = dk.astype(BF16)
        dv_s[pl.ds(k0, TK), :] = dv.astype(BF16)
        return 0

    lax.fori_loop(0, NK // TK, one_chunk, 0)
    place4 = [shift(HD, cols, 0, dst) for _, cols, dst in WINDOWS]
    half = ROWS // 2
    for n, ref in enumerate(dkv_refs):
        base = n * ROWS
        parts = [
            mm((dk_s, dv_s)[i % 2][base + i // 2 * half : base + (i // 2 + 1) * half, :HD], place4[i]) for i in range(4)
        ]
        for k, piece in enumerate(pack_four(parts)):
            ref[:, :, k * 128 : (k + 1) * 128] = piece.reshape(N_G, HALF, 128)
    for n in range(N_Z):
        ref, row = dq_refs[n % 2], n // 2 * PENCIL
        parts = []
        for quarter in range(4):
            r0 = n * ROWS + quarter // 2 * half
            x = mm(dq_s[:, r0 : r0 + half].astype(BF16), place4[quarter], CONTRACT_FIRST)
            x = x.reshape(N_G, 2, PENCIL, x.shape[1])[:, quarter % 2]
            parts.append(x.reshape(N_G * PENCIL, x.shape[2]))
        for k, piece in enumerate(pack_four(parts)):
            ref[:, row : row + PENCIL, k * 128 : (k + 1) * 128] = piece.reshape(N_G, PENCIL, 128)


def grads(rows, statistics):
    return pl.pallas_call(
        grads_kernel,
        out_shape=[pltpu.VMEM((N_G, HALF, WIDE), BF16)] * 4,
        in_specs=[VMEM] * (5 + N_Z),
        out_specs=[VMEM] * 4,
        scratch_shapes=[pltpu.VMEM((HD, NQ), F32)]
        + [pltpu.VMEM((NK, 128), BF16)] * 2
        + [pltpu.VMEM((8, NQ), F32)] * 2,
        cost_estimate=pl.CostEstimate(flops=10 * NQ * NK * 256, transcendentals=NQ * NK, bytes_accessed=8 << 20),
        compiler_params=pltpu.CompilerParams(vmem_limit_bytes=40 << 20),
        name="grads",
    )(*here(*rows, *statistics))


def meet_kernel(mine_ref, theirs_ref, keep_ref, send_ref):
    total = mine_ref[...].astype(F32) + theirs_ref[...].astype(F32)
    keep_ref[...] = total[:, :PENCIL]
    send_ref[...] = total[:, PENCIL:].astype(BF16)


def meet(mine, theirs):
    return pl.pallas_call(
        meet_kernel,
        out_shape=(
            pltpu.VMEM((N_G, PENCIL, WIDE), F32),
            pltpu.VMEM((N_G, PENCIL, WIDE), BF16),
        ),
        in_specs=[VMEM, VMEM],
        out_specs=(VMEM, VMEM),
        compiler_params=pltpu.CompilerParams(vmem_limit_bytes=16 << 20),
        name="meet",
    )(*here(mine, theirs))


def combine_kernel(*refs):
    out_ref = refs[-1]
    row = 0
    for parts in (refs[:2], refs[2:-1]):
        total = (parts[0][...].astype(F32) + parts[1][...].astype(F32)).astype(BF16)
        out_ref[:, row : row + total.shape[1], :] = total
        row += total.shape[1]


def combine(parts):
    return pl.pallas_call(
        combine_kernel,
        out_shape=jax.ShapeDtypeStruct((N_G, HALF + PENCIL, WIDE), BF16),
        in_specs=[VMEM] * len(parts),
        out_specs=VMEM,
        compiler_params=pltpu.CompilerParams(vmem_limit_bytes=16 << 20),
        name="combine",
    )(*here(*parts))


def finish_kernel(got_ref, query_ref, key_ref, value_ref):
    for h in range(H):
        here = slice(h * HD, (h + 1) * HD)
        for half in range(2):
            lane = half * 2 * HD
            rows = slice(half * HALF, (half + 1) * HALF)
            key_ref[rows, here] = got_ref[h, :HALF, lane : lane + HD]
            value_ref[rows, here] = got_ref[h, :HALF, lane + HD : lane + 2 * HD]
        for quarter in range(4):
            rows = slice(quarter * PENCIL, (quarter + 1) * PENCIL)
            query_ref[rows, here] = got_ref[h, HALF:, quarter * HD : (quarter + 1) * HD]


def finish(got):
    return pl.pallas_call(
        finish_kernel,
        out_shape=[jax.ShapeDtypeStruct((PD, D), BF16)] * 3,
        in_specs=[VMEM],
        out_specs=[VMEM] * 3,
        compiler_params=pltpu.CompilerParams(vmem_limit_bytes=16 << 20),
        name="finish",
    )(got)


def over_a(x):
    return lax.ppermute(x, Z, ((0, 3), (3, 0), (1, 2), (2, 1)))


def over_b(x):
    return lax.ppermute(x, Z, ((0, 1), (1, 0), (2, 3), (3, 2)))


def over_core(x):
    return lax.ppermute(x, CORE, ((0, 1), (1, 0)))


def to_heads(x):
    return lax.all_to_all(x, HEADS, 0, 0, tiled=True)


def layer(obj_query, grad_out, pattern_key, pattern_value, pencil_order):
    place = jnp.stack(
        [lax.axis_index(BLK_GRP) * (PD // PENCIL), lax.axis_index(GRP) * (pattern_key.shape[0] // PENCIL)]
    ).astype(jnp.int32)
    sent = pack(pencil_order, place, obj_query, grad_out, pattern_key, pattern_value)
    got = to_heads(sent)
    queries, keys = [got[:, :HALF]], [got[:, HALF:]]
    queries.append(over_core(queries[0]))
    queries.append(over_b(queries[0]))
    keys.append(over_a(keys[0]))
    first = first_stats(queries[0], queries[1], keys[0])
    queries.append(over_core(queries[2]))
    statistics = [stats(queries[2], queries[3], keys[1], first)]
    third = over_b(statistics[0])
    statistics += [over_core(statistics[0]), third, over_core(third)]
    rows = rows_of(queries, keys)
    keys_here, keys_there, queries_here, queries_there = grads(rows, statistics)
    keys_got = over_a(keys_there)
    queries_got = over_core(queries_there)
    keep, send = meet(queries_here, queries_got)
    queries_got = over_b(send)
    total = combine([keys_here, keys_got, keep, queries_got])
    total = to_heads(total)
    return tuple(finish(total))


def solution(mesh):
    split = Mesh(mesh.devices.reshape(4, 2, 2, 4, 2), BLK_GRP)
    return jax.shard_map(
        layer,
        mesh=split,
        in_specs=(P(BLK_GRP, None), P(BLK_GRP, None), P(GRP, None), P(GRP, None), P()),
        out_specs=(P(BLK_GRP, None), P(BLK_GRP, None), P(BLK_GRP, None)),
        check_vma=False,
    )
```

```python
import functools
import math

import jax
import jax.numpy as jnp
from jax import lax
from jax.experimental import pallas as pl
from jax.experimental.pallas import tpu as pltpu
from jax.sharding import Mesh
from jax.sharding import PartitionSpec as P


D = 1536
H = 16
HD = D // H
PENCIL = 16
PD = 64
HALF = PD // 2
WIDE = 4 * HD
N_Z = 4
N_G = 16
BLK_GRP = ("blk_0", "blk_1", "grp_0", "grp_1", "grp_2")
GRP = ("grp_0", "grp_1", "grp_2")
HEADS = ("blk_1", "grp_0", "grp_1")
Z = "blk_0"
CORE = "grp_2"
SCALE = 1.0 / math.sqrt(HD)
C2 = SCALE * math.log2(math.e)
TK = 512
SUB = 64
NEG = -1e30
F32 = jnp.float32
BF16 = jnp.bfloat16
CONTRACT_LAST = (((1,), (1,)), ((), ()))
CONTRACT_FIRST = (((0,), (0,)), ((), ()))
ROWS = N_G * PD
NQ = N_Z * ROWS
NK = 2 * ROWS
VMEM = pl.BlockSpec(memory_space=pltpu.VMEM)


def here(*arrays):
    return [pltpu.with_memory_space_constraint(x, pltpu.VMEM) for x in arrays]


def away(x):
    return pltpu.with_memory_space_constraint(x, pltpu.HBM)


WINDOWS = ((0, 128, 0), (0, 256, HD), (128, 256, 2 * HD - 128), (256, 128, 3 * HD - 256))


def mm(a, b, dims=(((1,), (0,)), ((), ()))):
    return lax.dot_general(a, b, dims, preferred_element_type=F32)


def shift(rows, cols, src, dst):
    i = lax.broadcasted_iota(jnp.int32, (rows, cols), 0) - src
    j = lax.broadcasted_iota(jnp.int32, (rows, cols), 1) - dst
    return jnp.where((i == j) & (i >= 0) & (i < HD), 1.0, 0.0).astype(BF16)


def turned_shift(cols, src):
    i = lax.broadcasted_iota(jnp.int32, (128, cols), 0)
    j = lax.broadcasted_iota(jnp.int32, (128, cols), 1) - src
    return jnp.where((i == j) & (i < HD), 1.0, 0.0).astype(BF16)


def pack_four(parts):
    a, b, c, d = parts
    return (
        (a + b[:, :128]).astype(BF16),
        (b[:, 128:] + c[:, :128]).astype(BF16),
        (c[:, 128:] + d).astype(BF16),
    )


def pack_kernel(order_ref, place_ref, q_ref, g_ref, k_ref, v_ref, out_ref, a_s, b_s):
    i = pl.program_id(0)
    at = pl.ds(pl.multiple_of(i // 2 * PD + HALF + i % 2 * PENCIL, PENCIL), PENCIL)
    a_s[at, :] = k_ref[...]
    b_s[at, :] = v_ref[...]

    @pl.when(i == PD // PENCIL - 1)
    def _():
        for half in range(2):
            rows = slice(half * HALF, (half + 1) * HALF)
            a_s[half * PD : half * PD + HALF, :] = q_ref[rows, :]
            b_s[half * PD : half * PD + HALF, :] = g_ref[rows, :]
        for turn in range(4):
            heads = range(turn, H, 4)
            offset = turn * HD % 128
            width = 128 if offset + HD <= 128 else 256
            parts = []
            for n, (_, cols, dst) in enumerate(WINDOWS):
                ref = (a_s, b_s)[n % 2]
                rows = slice(n // 2 * PD, (n // 2 + 1) * PD)
                x = [ref[rows, h * HD // 128 * 128 : h * HD // 128 * 128 + width] for h in heads]
                parts.append(mm(jnp.concatenate(x, axis=0), shift(width, cols, offset, dst)))
            for n, piece in enumerate(pack_four(parts)):
                for k, h in enumerate(heads):
                    out_ref[h, :, n * 128 : (n + 1) * 128] = piece[k * PD : (k + 1) * PD]


def pack(order, place, obj_query, grad_out, pattern_key, pattern_value):
    rows = pl.BlockSpec((PD, D), lambda i, order, place: (0, 0))
    block = pl.BlockSpec((PENCIL, D), lambda i, order, place: (order[place[0] + i] - place[1], 0))
    return pl.pallas_call(
        pack_kernel,
        out_shape=jax.ShapeDtypeStruct((H, PD, WIDE), BF16),
        grid_spec=pltpu.PrefetchScalarGridSpec(
            num_scalar_prefetch=2,
            grid=(PD // PENCIL,),
            in_specs=[rows, rows, block, block],
            out_specs=pl.BlockSpec((H, PD, WIDE), lambda i, order, place: (0, 0, 0)),
            scratch_shapes=[pltpu.VMEM((2 * PD, D), BF16)] * 2,
        ),
        compiler_params=pltpu.CompilerParams(vmem_limit_bytes=16 << 20),
        name="pack",
    )(away(order), place, *map(away, (obj_query, grad_out, pattern_key, pattern_value)))


def unpack(ref, stores, turned=False):
    half = ROWS // 2
    for n, (start, width, offset) in enumerate(WINDOWS):
        out, base = stores[n % 2]
        if out is None:
            continue
        at = slice(base + n // 2 * half, base + n // 2 * half + half)
        x = ref[:, :, start : start + width].reshape(half, width)
        if turned:
            out[:, at] = mm(turned_shift(width, offset), x, CONTRACT_LAST)[: out.shape[0]].astype(BF16)
        else:
            out[at, :] = mm(x, shift(width, 128, offset, 0)).astype(BF16)


def sweep(state, k_ref, v_ref, qt, gt):
    m, l, w = state
    rows, cols = k_ref.shape[0], qt.shape[1]
    s = mm(k_ref[...], qt).reshape(rows // SUB, SUB // 8, 8, cols)
    d = mm(v_ref[...], gt).reshape(rows // SUB, SUB // 8, 8, cols)
    for i in range(rows // SUB):
        top = jnp.maximum(m, jnp.max(s[i], axis=0))
        fade = jnp.exp2((m - top) * C2)
        e = jnp.exp2((s[i] - top[None]) * C2)
        m, l, w = top, l * fade + jnp.sum(e, axis=0), w * fade + jnp.sum(e * d[i], axis=0)
    return m, l, w


def write_stats(st_ref, n, state):
    m, l, w = state
    top = jnp.max(m, axis=0, keepdims=True)
    fade = jnp.exp2((m - top) * C2)
    row, cols = n // 2 * 4, slice(n % 2 * ROWS, (n % 2 + 1) * ROWS)
    st_ref[row : row + 1, cols] = top
    st_ref[row + 1 : row + 2, cols] = jnp.sum(l * fade, axis=0, keepdims=True)
    st_ref[row + 2 : row + 3, cols] = jnp.sum(w * fade, axis=0, keepdims=True)


def first_stats_kernel(qa_ref, qb_ref, kv_ref, st_ref, q_ref, g_ref, k_ref, v_ref):
    unpack(kv_ref, ((k_ref, 0), (v_ref, 0)))
    for n, ref in enumerate((qa_ref, qb_ref)):
        unpack(ref, ((q_ref, n * ROWS), (g_ref, n * ROWS)), turned=True)
    st_ref[...] = jnp.zeros_like(st_ref)
    for n in range(2):
        here = slice(n * ROWS, (n + 1) * ROWS)
        zero = jnp.zeros((8, ROWS), F32)
        state = (jnp.full((8, ROWS), NEG, F32), zero, zero)
        write_stats(st_ref, n, sweep(state, k_ref, v_ref, q_ref[:, here], g_ref[:, here]))


def first_stats(qa, qb, kv):
    return pl.pallas_call(
        first_stats_kernel,
        out_shape=[pltpu.VMEM((8, NQ // 2), F32)]
        + [pltpu.VMEM((128, 2 * ROWS), BF16)] * 2
        + [pltpu.VMEM((ROWS, 128), BF16)] * 2,
        in_specs=[VMEM] * 3,
        out_specs=[VMEM] * 5,
        cost_estimate=pl.CostEstimate(flops=NQ * NK * 256, transcendentals=NQ * NK // 4, bytes_accessed=2 << 20),
        compiler_params=pltpu.CompilerParams(vmem_limit_bytes=32 << 20),
        name="first_stats",
    )(*here(qa, qb, kv))


def stats_kernel(
    qa_ref, qb_ref, kv_ref, part_ref, q_own, g_own, k_own, v_own, st_ref, q_s, g_s, k_s, v_s
):
    unpack(kv_ref, ((k_s, 0), (v_s, 0)))
    for n, ref in enumerate((qa_ref, qb_ref)):
        unpack(ref, ((q_s, n * ROWS), (g_s, n * ROWS)), turned=True)
    st_ref[...] = jnp.zeros_like(st_ref)
    zero = jnp.zeros((8, ROWS), F32)
    for n in range(2):
        here = slice(n * ROWS, (n + 1) * ROWS)
        top, total, weighted = (part_ref[i : i + 1, here] for i in range(3))
        first = lax.broadcasted_iota(jnp.int32, (8, ROWS), 0) == 0
        state = (zero + top, jnp.where(first, total, zero), jnp.where(first, weighted, zero))
        write_stats(st_ref, n, sweep(state, k_s, v_s, q_own[:, here], g_own[:, here]))
    for n in range(2):
        here = slice(n * ROWS, (n + 1) * ROWS)
        qt, gt = q_s[:, here], g_s[:, here]
        state = sweep((jnp.full((8, ROWS), NEG, F32), zero, zero), k_own, v_own, qt, gt)
        write_stats(st_ref, 2 + n, sweep(state, k_s, v_s, qt, gt))


def stats(qa, qb, kv, first):
    return pl.pallas_call(
        stats_kernel,
        out_shape=pltpu.VMEM((8, NQ // 2), F32),
        in_specs=[VMEM] * 8,
        out_specs=VMEM,
        scratch_shapes=[pltpu.VMEM((128, 2 * ROWS), BF16)] * 2 + [pltpu.VMEM((ROWS, 128), BF16)] * 2,
        cost_estimate=pl.CostEstimate(flops=3 * NQ * NK * 256, transcendentals=NQ * NK, bytes_accessed=4 << 20),
        compiler_params=pltpu.CompilerParams(vmem_limit_bytes=36 << 20),
        name="stats",
    )(*here(qa, qb, kv, *first))


def rows_kernel(*refs):
    q_refs, kv_refs = refs[:N_Z], refs[N_Z : N_Z + 2]
    q_s, g_s, k_s, v_s, t_s = refs[N_Z + 2 :]
    for n, ref in enumerate(kv_refs):
        unpack(ref, ((k_s, n * ROWS), (v_s, n * ROWS)))
        unpack(ref, ((t_s, n * ROWS), (None, 0)), turned=True)
    for n, ref in enumerate(q_refs):
        unpack(ref, ((q_s, n * ROWS), (g_s, n * ROWS)))


def rows_of(queries, keys):
    return pl.pallas_call(
        rows_kernel,
        out_shape=[pltpu.VMEM((NQ, 128), BF16)] * 2
        + [pltpu.VMEM((NK, 128), BF16)] * 2
        + [pltpu.VMEM((HD, NK), BF16)],
        in_specs=[VMEM] * (N_Z + 2),
        out_specs=[VMEM] * 5,
        compiler_params=pltpu.CompilerParams(vmem_limit_bytes=24 << 20),
        name="rows_of",
    )(*here(*queries, *keys))


def block_of(ref, n):
    row, col = n // 2 * 4, n % 2 * ROWS
    return [ref[row + i : row + i + 1, col : col + ROWS] for i in range(3)]


def joined(parts):
    top = functools.reduce(jnp.maximum, [part[0] for part in parts])
    fades = [jnp.exp2((part[0] - top) * C2) for part in parts]
    total = sum(part[1] * fade for part, fade in zip(parts, fades))
    weighted = sum(part[2] * fade for part, fade in zip(parts, fades))
    return top * C2 + jnp.log2(total), weighted / total


def grads_kernel(key_block, blocks, takes_dq, takes_dkv, gives_dq, gives_dkv, *refs):
    refs = list(refs)
    q_s, g_s, k_s, v_s, t_s = refs[:5]
    st_refs, refs = refs[5 : 5 + N_Z], refs[5 + N_Z :]
    dq_in = refs.pop(0) if takes_dq else None
    dk_in, dv_in = (refs.pop(0), refs.pop(0)) if takes_dkv else (None, None)
    dq_outs = [refs.pop(0) for _ in (range(1) if gives_dq else blocks)]
    dkv_outs = [refs.pop(0) for _ in range(1 if gives_dkv else 2)]
    dq_s, dk_s, dv_s, log_s, mean_s = refs
    if gives_dq:
        dq_s = dq_outs[0]
    if not gives_dkv:
        dk_s, dv_s = dkv_outs
    for i, n in enumerate(blocks):
        log_now, mean_now = joined([block_of(st, n ^ t) for t, st in enumerate(st_refs)])
        here = slice(i * ROWS, (i + 1) * ROWS)
        log_s[:, here] = jnp.broadcast_to(log_now, (8, ROWS))
        mean_s[:, here] = jnp.broadcast_to(mean_now, (8, ROWS))
        dq_s[:, here] = dq_in[:, n * ROWS : (n + 1) * ROWS] if takes_dq else jnp.zeros((HD, ROWS), F32)

    def one_chunk(j, _):
        j0 = pl.multiple_of(j * TK, TK)
        k0 = pl.multiple_of(key_block * ROWS + j * TK, TK)
        kc = k_s[pl.ds(k0, TK), :]
        vc = v_s[pl.ds(k0, TK), :]
        kt = t_s[:, pl.ds(k0, TK)]
        if takes_dkv:
            dk, dv = dk_in[pl.ds(j0, TK), :], dv_in[pl.ds(j0, TK), :]
        else:
            dk = dv = jnp.zeros((TK, 128), F32)
        for i, n in enumerate(blocks):
            here = slice(i * ROWS, (i + 1) * ROWS)
            qt = q_s[n * ROWS : (n + 1) * ROWS, :]
            gt = g_s[n * ROWS : (n + 1) * ROWS, :]
            s = mm(kc, qt, CONTRACT_LAST).reshape(TK // 8, 8, ROWS)
            d = mm(vc, gt, CONTRACT_LAST).reshape(TK // 8, 8, ROWS)
            p = jnp.exp2(s * C2 - log_s[:, here][None])
            sg = ((d - mean_s[:, here][None]) * (p * SCALE)).astype(BF16).reshape(TK, ROWS)
            p = p.astype(BF16).reshape(TK, ROWS)
            dq_s[:, here] += mm(kt, sg)
            dk, dv = dk + mm(sg, qt), dv + mm(p, gt)
        dk_s[pl.ds(j0, TK), :] = dk.astype(dk_s.dtype)
        dv_s[pl.ds(j0, TK), :] = dv.astype(dv_s.dtype)
        return 0

    lax.fori_loop(0, ROWS // TK, one_chunk, 0, unroll=len(blocks) == 1)
    place4 = [shift(HD, cols, 0, dst) for _, cols, dst in WINDOWS]
    half = ROWS // 2
    if gives_dkv:
        parts = [mm((dk_s, dv_s)[i % 2][i // 2 * half : (i // 2 + 1) * half, :HD], place4[i]) for i in range(4)]
        for k, piece in enumerate(pack_four(parts)):
            dkv_outs[0][:, :, k * 128 : (k + 1) * 128] = piece.reshape(N_G, HALF, 128)
    if not gives_dq:
        for i, ref in enumerate(dq_outs):
            parts = []
            for quarter in range(4):
                r0 = i * ROWS + quarter // 2 * half
                x = mm(dq_s[:, r0 : r0 + half].astype(BF16), place4[quarter], CONTRACT_FIRST)
                x = x.reshape(N_G, 2, PENCIL, x.shape[1])[:, quarter % 2]
                parts.append(x.reshape(N_G * PENCIL, x.shape[2]))
            for k, piece in enumerate(pack_four(parts)):
                ref[:, :, k * 128 : (k + 1) * 128] = piece.reshape(N_G, PENCIL, 128)


def grads(key_block, blocks, rows, statistics, dq=None, dkv=None, gives_dq=False, gives_dkv=True):
    taken = [*(() if dq is None else (dq,)), *(() if dkv is None else dkv)]
    size = len(blocks) * ROWS
    dq_out = [pltpu.VMEM((HD, size), F32)] if gives_dq else [pltpu.VMEM((N_G, PENCIL, WIDE), BF16)] * len(blocks)
    dkv_out = [pltpu.VMEM((N_G, HALF, WIDE), BF16)] if gives_dkv else [pltpu.VMEM((ROWS, 128), F32)] * 2
    return pl.pallas_call(
        functools.partial(grads_kernel, key_block, blocks, dq is not None, dkv is not None, gives_dq, gives_dkv),
        out_shape=dq_out + dkv_out,
        in_specs=[VMEM] * (5 + N_Z + len(taken)),
        out_specs=[VMEM] * len(dq_out + dkv_out),
        scratch_shapes=[pltpu.VMEM((8, 128) if gives_dq else (HD, size), F32)]
        + [pltpu.VMEM((ROWS, 128), BF16)] * 2
        + [pltpu.VMEM((8, size), F32)] * 2,
        cost_estimate=pl.CostEstimate(
            flops=10 * size * ROWS * 256, transcendentals=size * ROWS, bytes_accessed=1 << 20
        ),
        compiler_params=pltpu.CompilerParams(vmem_limit_bytes=40 << 20),
    )(*here(*rows, *statistics, *taken))


def meet_kernel(mine_ref, theirs_ref, send_ref):
    send_ref[...] = (mine_ref[...].astype(F32) + theirs_ref[...].astype(F32)).astype(BF16)


def meet(mine, theirs):
    return pl.pallas_call(
        meet_kernel,
        out_shape=pltpu.VMEM((N_G, PENCIL, WIDE), BF16),
        in_specs=[VMEM, VMEM],
        out_specs=VMEM,
        compiler_params=pltpu.CompilerParams(vmem_limit_bytes=16 << 20),
        name="meet",
    )(*here(mine, theirs))


def combine_kernel(*refs):
    out_ref = refs[-1]
    row = 0
    for parts in (refs[:2], refs[2:-1]):
        total = parts[0][...].astype(F32)
        for part in parts[1:]:
            total = total + part[...].astype(F32)
        out_ref[:, row : row + total.shape[1], :] = total.astype(BF16)
        row += total.shape[1]


def combine(parts):
    return pl.pallas_call(
        combine_kernel,
        out_shape=jax.ShapeDtypeStruct((N_G, HALF + PENCIL, WIDE), BF16),
        in_specs=[VMEM] * len(parts),
        out_specs=VMEM,
        compiler_params=pltpu.CompilerParams(vmem_limit_bytes=16 << 20),
        name="combine",
    )(*here(*parts))


def finish_kernel(got_ref, query_ref, key_ref, value_ref):
    for h in range(H):
        here = slice(h * HD, (h + 1) * HD)
        for half in range(2):
            lane = half * 2 * HD
            rows = slice(half * HALF, (half + 1) * HALF)
            key_ref[rows, here] = got_ref[h, :HALF, lane : lane + HD]
            value_ref[rows, here] = got_ref[h, :HALF, lane + HD : lane + 2 * HD]
        for quarter in range(4):
            rows = slice(quarter * PENCIL, (quarter + 1) * PENCIL)
            query_ref[rows, here] = got_ref[h, HALF:, quarter * HD : (quarter + 1) * HD]


def finish(got):
    return pl.pallas_call(
        finish_kernel,
        out_shape=[jax.ShapeDtypeStruct((PD, D), BF16)] * 3,
        in_specs=[VMEM],
        out_specs=[VMEM] * 3,
        compiler_params=pltpu.CompilerParams(vmem_limit_bytes=16 << 20),
        name="finish",
    )(got)


def over_a(x):
    return lax.ppermute(x, Z, ((0, 3), (3, 0), (1, 2), (2, 1)))


def over_b(x):
    return lax.ppermute(x, Z, ((0, 1), (1, 0), (2, 3), (3, 2)))


def over_core(x):
    return lax.ppermute(x, CORE, ((0, 1), (1, 0)))


def to_heads(x):
    return lax.all_to_all(x, HEADS, 0, 0, tiled=True)


def layer(obj_query, grad_out, pattern_key, pattern_value, pencil_order):
    place = jnp.stack(
        [lax.axis_index(BLK_GRP) * (PD // PENCIL), lax.axis_index(GRP) * (pattern_key.shape[0] // PENCIL)]
    ).astype(jnp.int32)
    sent = pack(pencil_order, place, obj_query, grad_out, pattern_key, pattern_value)
    got = to_heads(sent)
    queries, keys = [got[:, :HALF]], [got[:, HALF:]]
    queries.append(over_core(queries[0]))
    queries.append(over_b(queries[0]))
    keys.append(over_a(keys[0]))
    first = first_stats(queries[0], queries[1], keys[0])
    queries.append(over_core(queries[2]))
    statistics = [stats(queries[2], queries[3], keys[1], first)]
    third = over_b(statistics[0])
    statistics += [over_core(statistics[0]), third, over_core(third)]
    rows = rows_of(queries, keys)
    dq, keys_there = grads(1, (0, 1, 2, 3), rows, statistics, gives_dq=True)
    keys_got = over_a(keys_there)
    core, beside, both, *dkv = grads(0, (1, 2, 3), rows, statistics, dq, gives_dkv=False)
    core_got, both_got = over_core(core), over_core(both)
    send = meet(beside, both_got)
    beside_got = over_b(send)
    own, keys_here = grads(0, (0,), rows, statistics, dq, dkv)
    total = combine([keys_here, keys_got, own, core_got, beside_got])
    total = to_heads(total)
    return tuple(finish(total))


def solution(mesh):
    split = Mesh(mesh.devices.reshape(4, 2, 2, 4, 2), BLK_GRP)
    return jax.shard_map(
        layer,
        mesh=split,
        in_specs=(P(BLK_GRP, None), P(BLK_GRP, None), P(GRP, None), P(GRP, None), P()),
        out_specs=(P(BLK_GRP, None), P(BLK_GRP, None), P(BLK_GRP, None)),
        check_vma=False,
    )
```

```python
import functools
import math

import jax
import jax.numpy as jnp
from jax import lax
from jax.experimental import pallas as pl
from jax.experimental.pallas import tpu as pltpu
from jax.sharding import Mesh
from jax.sharding import PartitionSpec as P


D = 1536
H = 16
HD = D // H
PENCIL = 16
PD = 64
HALF = PD // 2
WIDE = 4 * HD
N_Z = 4
N_G = 16
BLK_GRP = ("blk_0", "blk_1", "grp_0", "grp_1", "grp_2")
GRP = ("grp_0", "grp_1", "grp_2")
HEADS = ("blk_1", "grp_0", "grp_1")
Z = "blk_0"
CORE = "grp_2"
SCALE = 1.0 / math.sqrt(HD)
C2 = SCALE * math.log2(math.e)
TK = 512
SUB = 64
NEG = -1e30
F32 = jnp.float32
BF16 = jnp.bfloat16
CONTRACT_LAST = (((1,), (1,)), ((), ()))
CONTRACT_FIRST = (((0,), (0,)), ((), ()))
ROWS = N_G * PD
NQ = N_Z * ROWS
NK = 2 * ROWS
VMEM = pl.BlockSpec(memory_space=pltpu.VMEM)


def here(*arrays):
    return [pltpu.with_memory_space_constraint(x, pltpu.VMEM) for x in arrays]


def away(x):
    return pltpu.with_memory_space_constraint(x, pltpu.HBM)


WINDOWS = ((0, 128, 0), (0, 256, HD), (128, 256, 2 * HD - 128), (256, 128, 3 * HD - 256))


def mm(a, b, dims=(((1,), (0,)), ((), ()))):
    return lax.dot_general(a, b, dims, preferred_element_type=F32)


def shift(rows, cols, src, dst):
    i = lax.broadcasted_iota(jnp.int32, (rows, cols), 0) - src
    j = lax.broadcasted_iota(jnp.int32, (rows, cols), 1) - dst
    return jnp.where((i == j) & (i >= 0) & (i < HD), 1.0, 0.0).astype(BF16)


def turned_shift(cols, src):
    i = lax.broadcasted_iota(jnp.int32, (128, cols), 0)
    j = lax.broadcasted_iota(jnp.int32, (128, cols), 1) - src
    return jnp.where((i == j) & (i < HD), 1.0, 0.0).astype(BF16)


def pack_four(parts):
    a, b, c, d = parts
    return (
        (a + b[:, :128]).astype(BF16),
        (b[:, 128:] + c[:, :128]).astype(BF16),
        (c[:, 128:] + d).astype(BF16),
    )


def pack_kernel(order_ref, place_ref, q_ref, g_ref, k_ref, v_ref, out_ref, a_s, b_s):
    i = pl.program_id(0)
    at = pl.ds(pl.multiple_of(i // 2 * PD + HALF + i % 2 * PENCIL, PENCIL), PENCIL)
    a_s[at, :] = k_ref[...]
    b_s[at, :] = v_ref[...]

    @pl.when(i == PD // PENCIL - 1)
    def _():
        for half in range(2):
            rows = slice(half * HALF, (half + 1) * HALF)
            a_s[half * PD : half * PD + HALF, :] = q_ref[rows, :]
            b_s[half * PD : half * PD + HALF, :] = g_ref[rows, :]
        for turn in range(4):
            heads = range(turn, H, 4)
            offset = turn * HD % 128
            width = 128 if offset + HD <= 128 else 256
            parts = []
            for n, (_, cols, dst) in enumerate(WINDOWS):
                ref = (a_s, b_s)[n % 2]
                rows = slice(n // 2 * PD, (n // 2 + 1) * PD)
                x = [ref[rows, h * HD // 128 * 128 : h * HD // 128 * 128 + width] for h in heads]
                parts.append(mm(jnp.concatenate(x, axis=0), shift(width, cols, offset, dst)))
            for n, piece in enumerate(pack_four(parts)):
                for k, h in enumerate(heads):
                    out_ref[h, :, n * 128 : (n + 1) * 128] = piece[k * PD : (k + 1) * PD]


def pack(order, place, obj_query, grad_out, pattern_key, pattern_value):
    rows = pl.BlockSpec((PD, D), lambda i, order, place: (0, 0))
    block = pl.BlockSpec((PENCIL, D), lambda i, order, place: (order[place[0] + i] - place[1], 0))
    return pl.pallas_call(
        pack_kernel,
        out_shape=jax.ShapeDtypeStruct((H, PD, WIDE), BF16),
        grid_spec=pltpu.PrefetchScalarGridSpec(
            num_scalar_prefetch=2,
            grid=(PD // PENCIL,),
            in_specs=[rows, rows, block, block],
            out_specs=pl.BlockSpec((H, PD, WIDE), lambda i, order, place: (0, 0, 0)),
            scratch_shapes=[pltpu.VMEM((2 * PD, D), BF16)] * 2,
        ),
        compiler_params=pltpu.CompilerParams(vmem_limit_bytes=16 << 20),
        name="pack",
    )(away(order), place, *map(away, (obj_query, grad_out, pattern_key, pattern_value)))


def unpack(ref, stores, turned=False):
    half = ROWS // 2
    for n, (start, width, offset) in enumerate(WINDOWS):
        out, base = stores[n % 2]
        if out is None:
            continue
        at = slice(base + n // 2 * half, base + n // 2 * half + half)
        x = ref[:, :, start : start + width].reshape(half, width)
        if turned:
            out[:, at] = mm(turned_shift(width, offset), x, CONTRACT_LAST)[: out.shape[0]].astype(BF16)
        else:
            out[at, :] = mm(x, shift(width, 128, offset, 0)).astype(BF16)


def sweep(state, k_ref, v_ref, qt, gt):
    m, l, w = state
    rows, cols = k_ref.shape[0], qt.shape[1]
    s = mm(k_ref[...], qt).reshape(rows // SUB, SUB // 8, 8, cols)
    d = mm(v_ref[...], gt).reshape(rows // SUB, SUB // 8, 8, cols)
    for i in range(rows // SUB):
        top = jnp.maximum(m, jnp.max(s[i], axis=0))
        fade = jnp.exp2((m - top) * C2)
        e = jnp.exp2((s[i] - top[None]) * C2)
        m, l, w = top, l * fade + jnp.sum(e, axis=0), w * fade + jnp.sum(e * d[i], axis=0)
    return m, l, w


def write_stats(st_ref, n, state):
    m, l, w = state
    top = jnp.max(m, axis=0, keepdims=True)
    fade = jnp.exp2((m - top) * C2)
    row, cols = n // 2 * 4, slice(n % 2 * ROWS, (n % 2 + 1) * ROWS)
    st_ref[row : row + 1, cols] = top
    st_ref[row + 1 : row + 2, cols] = jnp.sum(l * fade, axis=0, keepdims=True)
    st_ref[row + 2 : row + 3, cols] = jnp.sum(w * fade, axis=0, keepdims=True)


def first_stats_kernel(qa_ref, qb_ref, kv_ref, st_ref, q_ref, g_ref, k_ref, v_ref):
    unpack(kv_ref, ((k_ref, 0), (v_ref, 0)))
    for n, ref in enumerate((qa_ref, qb_ref)):
        unpack(ref, ((q_ref, n * ROWS), (g_ref, n * ROWS)), turned=True)
    st_ref[...] = jnp.zeros_like(st_ref)
    for n in range(2):
        here = slice(n * ROWS, (n + 1) * ROWS)
        zero = jnp.zeros((8, ROWS), F32)
        state = (jnp.full((8, ROWS), NEG, F32), zero, zero)
        write_stats(st_ref, n, sweep(state, k_ref, v_ref, q_ref[:, here], g_ref[:, here]))


def first_stats(qa, qb, kv):
    return pl.pallas_call(
        first_stats_kernel,
        out_shape=[pltpu.VMEM((8, NQ // 2), F32)]
        + [pltpu.VMEM((128, 2 * ROWS), BF16)] * 2
        + [pltpu.VMEM((ROWS, 128), BF16)] * 2,
        in_specs=[VMEM] * 3,
        out_specs=[VMEM] * 5,
        cost_estimate=pl.CostEstimate(flops=NQ * NK * 256, transcendentals=NQ * NK // 4, bytes_accessed=2 << 20),
        compiler_params=pltpu.CompilerParams(vmem_limit_bytes=32 << 20),
        name="first_stats",
    )(*here(qa, qb, kv))


def stats_kernel(
    qa_ref, qb_ref, kv_ref, part_ref, q_own, g_own, k_own, v_own, st_ref, q_s, g_s, k_s, v_s
):
    unpack(kv_ref, ((k_s, 0), (v_s, 0)))
    for n, ref in enumerate((qa_ref, qb_ref)):
        unpack(ref, ((q_s, n * ROWS), (g_s, n * ROWS)), turned=True)
    st_ref[...] = jnp.zeros_like(st_ref)
    zero = jnp.zeros((8, ROWS), F32)
    for n in range(2):
        here = slice(n * ROWS, (n + 1) * ROWS)
        top, total, weighted = (part_ref[i : i + 1, here] for i in range(3))
        first = lax.broadcasted_iota(jnp.int32, (8, ROWS), 0) == 0
        state = (zero + top, jnp.where(first, total, zero), jnp.where(first, weighted, zero))
        write_stats(st_ref, n, sweep(state, k_s, v_s, q_own[:, here], g_own[:, here]))
    for n in range(2):
        here = slice(n * ROWS, (n + 1) * ROWS)
        qt, gt = q_s[:, here], g_s[:, here]
        state = sweep((jnp.full((8, ROWS), NEG, F32), zero, zero), k_own, v_own, qt, gt)
        write_stats(st_ref, 2 + n, sweep(state, k_s, v_s, qt, gt))


def stats(qa, qb, kv, first):
    return pl.pallas_call(
        stats_kernel,
        out_shape=pltpu.VMEM((8, NQ // 2), F32),
        in_specs=[VMEM] * 8,
        out_specs=VMEM,
        scratch_shapes=[pltpu.VMEM((128, 2 * ROWS), BF16)] * 2 + [pltpu.VMEM((ROWS, 128), BF16)] * 2,
        cost_estimate=pl.CostEstimate(flops=3 * NQ * NK * 256, transcendentals=NQ * NK, bytes_accessed=4 << 20),
        compiler_params=pltpu.CompilerParams(vmem_limit_bytes=36 << 20),
        name="stats",
    )(*here(qa, qb, kv, *first))


def rows_kernel(*refs):
    q_refs, kv_refs = refs[:N_Z], refs[N_Z : N_Z + 2]
    q_s, g_s, k_s, v_s, t_s = refs[N_Z + 2 :]
    for n, ref in enumerate(kv_refs):
        unpack(ref, ((k_s, n * ROWS), (v_s, n * ROWS)))
        unpack(ref, ((t_s, n * ROWS), (None, 0)), turned=True)
    for n, ref in enumerate(q_refs):
        unpack(ref, ((q_s, n * ROWS), (g_s, n * ROWS)))


def rows_of(queries, keys):
    return pl.pallas_call(
        rows_kernel,
        out_shape=[pltpu.VMEM((NQ, 128), BF16)] * 2
        + [pltpu.VMEM((NK, 128), BF16)] * 2
        + [pltpu.VMEM((HD, NK), BF16)],
        in_specs=[VMEM] * (N_Z + 2),
        out_specs=[VMEM] * 5,
        compiler_params=pltpu.CompilerParams(vmem_limit_bytes=24 << 20),
        name="rows_of",
    )(*here(*queries, *keys))


def block_of(ref, n):
    row, col = n // 2 * 4, n % 2 * ROWS
    return [ref[row + i : row + i + 1, col : col + ROWS] for i in range(3)]


def joined(parts):
    top = functools.reduce(jnp.maximum, [part[0] for part in parts])
    fades = [jnp.exp2((part[0] - top) * C2) for part in parts]
    total = sum(part[1] * fade for part, fade in zip(parts, fades))
    weighted = sum(part[2] * fade for part, fade in zip(parts, fades))
    return top * C2 + jnp.log2(total), weighted / total


def grads_kernel(key_block, blocks, takes_dq, takes_dkv, gives_dq, gives_dkv, *refs):
    refs = list(refs)
    q_s, g_s, k_s, v_s, t_s = refs[:5]
    st_refs, refs = refs[5 : 5 + N_Z], refs[5 + N_Z :]
    dq_in = refs.pop(0) if takes_dq else None
    dk_in, dv_in = (refs.pop(0), refs.pop(0)) if takes_dkv else (None, None)
    dq_outs = [refs.pop(0) for _ in (range(1) if gives_dq else blocks)]
    dkv_outs = [refs.pop(0) for _ in range(1 if gives_dkv else 2)]
    dq_s, dk_s, dv_s, log_s, mean_s = refs
    if gives_dq:
        dq_s = dq_outs[0]
    if not gives_dkv:
        dk_s, dv_s = dkv_outs
    for i, n in enumerate(blocks):
        log_now, mean_now = joined([block_of(st, n ^ t) for t, st in enumerate(st_refs)])
        here = slice(i * ROWS, (i + 1) * ROWS)
        log_s[:, here] = jnp.broadcast_to(log_now, (8, ROWS))
        mean_s[:, here] = jnp.broadcast_to(mean_now, (8, ROWS))
        dq_s[:, here] = dq_in[:, n * ROWS : (n + 1) * ROWS] if takes_dq else jnp.zeros((HD, ROWS), F32)

    def one_chunk(j, _):
        j0 = pl.multiple_of(j * TK, TK)
        k0 = pl.multiple_of(key_block * ROWS + j * TK, TK)
        kc = k_s[pl.ds(k0, TK), :]
        vc = v_s[pl.ds(k0, TK), :]
        kt = t_s[:, pl.ds(k0, TK)]
        if takes_dkv:
            dk, dv = dk_in[pl.ds(j0, TK), :], dv_in[pl.ds(j0, TK), :]
        else:
            dk = dv = jnp.zeros((TK, 128), F32)
        for i, n in enumerate(blocks):
            here = slice(i * ROWS, (i + 1) * ROWS)
            qt = q_s[n * ROWS : (n + 1) * ROWS, :]
            gt = g_s[n * ROWS : (n + 1) * ROWS, :]
            s = mm(kc, qt, CONTRACT_LAST).reshape(TK // 8, 8, ROWS)
            d = mm(vc, gt, CONTRACT_LAST).reshape(TK // 8, 8, ROWS)
            p = jnp.exp2(s * C2 - log_s[:, here][None])
            sg = ((d - mean_s[:, here][None]) * (p * SCALE)).astype(BF16).reshape(TK, ROWS)
            p = p.astype(BF16).reshape(TK, ROWS)
            dq_s[:, here] += mm(kt, sg)
            dk, dv = dk + mm(sg, qt), dv + mm(p, gt)
        dk_s[pl.ds(j0, TK), :] = dk.astype(dk_s.dtype)
        dv_s[pl.ds(j0, TK), :] = dv.astype(dv_s.dtype)
        return 0

    lax.fori_loop(0, ROWS // TK, one_chunk, 0, unroll=len(blocks) == 1)
    place4 = [shift(HD, cols, 0, dst) for _, cols, dst in WINDOWS]
    half = ROWS // 2
    if gives_dkv:
        parts = [mm((dk_s, dv_s)[i % 2][i // 2 * half : (i // 2 + 1) * half, :HD], place4[i]) for i in range(4)]
        for k, piece in enumerate(pack_four(parts)):
            dkv_outs[0][:, :, k * 128 : (k + 1) * 128] = piece.reshape(N_G, HALF, 128)
    if not gives_dq:
        for i, ref in enumerate(dq_outs):
            parts = []
            for quarter in range(4):
                r0 = i * ROWS + quarter // 2 * half
                x = mm(dq_s[:, r0 : r0 + half].astype(BF16), place4[quarter], CONTRACT_FIRST)
                x = x.reshape(N_G, 2, PENCIL, x.shape[1])[:, quarter % 2]
                parts.append(x.reshape(N_G * PENCIL, x.shape[2]))
            for k, piece in enumerate(pack_four(parts)):
                ref[:, :, k * 128 : (k + 1) * 128] = piece.reshape(N_G, PENCIL, 128)


def grads(key_block, blocks, rows, statistics, dq=None, dkv=None, gives_dq=False, gives_dkv=True):
    taken = [*(() if dq is None else (dq,)), *(() if dkv is None else dkv)]
    size = len(blocks) * ROWS
    dq_out = [pltpu.VMEM((HD, size), F32)] if gives_dq else [pltpu.VMEM((N_G, PENCIL, WIDE), BF16)] * len(blocks)
    dkv_out = [pltpu.VMEM((N_G, HALF, WIDE), BF16)] if gives_dkv else [pltpu.VMEM((ROWS, 128), F32)] * 2
    return pl.pallas_call(
        functools.partial(grads_kernel, key_block, blocks, dq is not None, dkv is not None, gives_dq, gives_dkv),
        out_shape=dq_out + dkv_out,
        in_specs=[VMEM] * (5 + N_Z + len(taken)),
        out_specs=[VMEM] * len(dq_out + dkv_out),
        scratch_shapes=[pltpu.VMEM((8, 128) if gives_dq else (HD, size), F32)]
        + [pltpu.VMEM((ROWS, 128), BF16)] * 2
        + [pltpu.VMEM((8, size), F32)] * 2,
        cost_estimate=pl.CostEstimate(
            flops=10 * size * ROWS * 256, transcendentals=size * ROWS, bytes_accessed=1 << 20
        ),
        compiler_params=pltpu.CompilerParams(vmem_limit_bytes=40 << 20),
    )(*here(*rows, *statistics, *taken))


def meet_kernel(mine_ref, theirs_ref, send_ref):
    send_ref[...] = (mine_ref[...].astype(F32) + theirs_ref[...].astype(F32)).astype(BF16)


def meet(mine, theirs):
    return pl.pallas_call(
        meet_kernel,
        out_shape=pltpu.VMEM((N_G, PENCIL, WIDE), BF16),
        in_specs=[VMEM, VMEM],
        out_specs=VMEM,
        compiler_params=pltpu.CompilerParams(vmem_limit_bytes=16 << 20),
        name="meet",
    )(*here(mine, theirs))


def combine_kernel(*refs):
    out_ref = refs[-1]
    row = 0
    for parts in (refs[:2], refs[2:-1]):
        total = parts[0][...].astype(F32)
        for part in parts[1:]:
            total = total + part[...].astype(F32)
        out_ref[:, row : row + total.shape[1], :] = total.astype(BF16)
        row += total.shape[1]


def combine(parts):
    return pl.pallas_call(
        combine_kernel,
        out_shape=jax.ShapeDtypeStruct((N_G, HALF + PENCIL, WIDE), BF16),
        in_specs=[VMEM] * len(parts),
        out_specs=VMEM,
        compiler_params=pltpu.CompilerParams(vmem_limit_bytes=16 << 20),
        name="combine",
    )(*here(*parts))


def finish_kernel(got_ref, query_ref, key_ref, value_ref):
    for h in range(H):
        here = slice(h * HD, (h + 1) * HD)
        for half in range(2):
            lane = half * 2 * HD
            rows = slice(half * HALF, (half + 1) * HALF)
            key_ref[rows, here] = got_ref[h, :HALF, lane : lane + HD]
            value_ref[rows, here] = got_ref[h, :HALF, lane + HD : lane + 2 * HD]
        for quarter in range(4):
            rows = slice(quarter * PENCIL, (quarter + 1) * PENCIL)
            query_ref[rows, here] = got_ref[h, HALF:, quarter * HD : (quarter + 1) * HD]


def finish(got):
    return pl.pallas_call(
        finish_kernel,
        out_shape=[jax.ShapeDtypeStruct((PD, D), BF16)] * 3,
        in_specs=[VMEM],
        out_specs=[VMEM] * 3,
        compiler_params=pltpu.CompilerParams(vmem_limit_bytes=16 << 20),
        name="finish",
    )(got)


def over_a(x):
    return lax.ppermute(x, Z, ((0, 3), (3, 0), (1, 2), (2, 1)))


def over_b(x):
    return lax.ppermute(x, Z, ((0, 1), (1, 0), (2, 3), (3, 2)))


def over_core(x):
    return lax.ppermute(x, CORE, ((0, 1), (1, 0)))


def over_b_and_core(x):
    near = (1, 0, 3, 2)
    pairs = tuple((2 * k + c, 2 * near[k] + 1 - c) for k in range(N_Z) for c in range(2))
    return lax.ppermute(x, (Z, CORE), pairs)


def to_heads(x):
    return lax.all_to_all(x, HEADS, 0, 0, tiled=True)


def layer(obj_query, grad_out, pattern_key, pattern_value, pencil_order):
    place = jnp.stack(
        [lax.axis_index(BLK_GRP) * (PD // PENCIL), lax.axis_index(GRP) * (pattern_key.shape[0] // PENCIL)]
    ).astype(jnp.int32)
    sent = pack(pencil_order, place, obj_query, grad_out, pattern_key, pattern_value)
    got = to_heads(sent)
    queries, keys = [got[:, :HALF]], [got[:, HALF:]]
    queries.append(over_core(queries[0]))
    queries.append(over_b(queries[0]))
    keys.append(over_a(keys[0]))
    first = first_stats(queries[0], queries[1], keys[0])
    queries.append(over_core(queries[2]))
    statistics = [stats(queries[2], queries[3], keys[1], first)]
    both = over_b_and_core(statistics[0])
    beside = over_b(statistics[0])
    statistics += [over_core(statistics[0]), beside, both]
    rows = rows_of(queries, keys)
    dq, keys_there = grads(1, (0, 1, 2, 3), rows, statistics, gives_dq=True)
    keys_got = over_a(keys_there)
    beside, both, *dkv = grads(0, (2, 3), rows, statistics, dq, gives_dkv=False)
    both_got = over_core(both)
    send = meet(beside, both_got)
    beside_got = over_b(send)
    own, core, keys_here = grads(0, (0, 1), rows, statistics, dq, dkv)
    core_got = over_core(core)
    total = combine([keys_here, keys_got, own, core_got, beside_got])
    total = to_heads(total)
    return tuple(finish(total))


def solution(mesh):
    split = Mesh(mesh.devices.reshape(4, 2, 2, 4, 2), BLK_GRP)
    return jax.shard_map(
        layer,
        mesh=split,
        in_specs=(P(BLK_GRP, None), P(BLK_GRP, None), P(GRP, None), P(GRP, None), P()),
        out_specs=(P(BLK_GRP, None), P(BLK_GRP, None), P(BLK_GRP, None)),
        check_vma=False,
    )
```

```python
import functools
import math

import jax
import jax.numpy as jnp
from jax import lax
from jax.experimental import pallas as pl
from jax.experimental.pallas import tpu as pltpu
from jax.sharding import Mesh
from jax.sharding import PartitionSpec as P


D = 1536
H = 16
HD = D // H
PENCIL = 16
PD = 64
HALF = PD // 2
WIDE = 4 * HD
N_Z = 4
N_G = 16
BLK_GRP = ("blk_0", "blk_1", "grp_0", "grp_1", "grp_2")
GRP = ("grp_0", "grp_1", "grp_2")
HEADS = ("blk_1", "grp_0", "grp_1")
Z = "blk_0"
CORE = "grp_2"
SCALE = 1.0 / math.sqrt(HD)
C2 = SCALE * math.log2(math.e)
TK = 512
SUB = 64
NEG = -1e30
F32 = jnp.float32
BF16 = jnp.bfloat16
CONTRACT_LAST = (((1,), (1,)), ((), ()))
CONTRACT_FIRST = (((0,), (0,)), ((), ()))
ROWS = N_G * PD
NQ = N_Z * ROWS
NK = 2 * ROWS
VMEM = pl.BlockSpec(memory_space=pltpu.VMEM)


def here(*arrays):
    return [pltpu.with_memory_space_constraint(x, pltpu.VMEM) for x in arrays]


def away(x):
    return pltpu.with_memory_space_constraint(x, pltpu.HBM)


WINDOWS = ((0, 128, 0), (0, 256, HD), (128, 256, 2 * HD - 128), (256, 128, 3 * HD - 256))


def mm(a, b, dims=(((1,), (0,)), ((), ()))):
    return lax.dot_general(a, b, dims, preferred_element_type=F32)


def shift(rows, cols, src, dst):
    i = lax.broadcasted_iota(jnp.int32, (rows, cols), 0) - src
    j = lax.broadcasted_iota(jnp.int32, (rows, cols), 1) - dst
    return jnp.where((i == j) & (i >= 0) & (i < HD), 1.0, 0.0).astype(BF16)


def turned_shift(cols, src):
    i = lax.broadcasted_iota(jnp.int32, (128, cols), 0)
    j = lax.broadcasted_iota(jnp.int32, (128, cols), 1) - src
    return jnp.where((i == j) & (i < HD), 1.0, 0.0).astype(BF16)


def pack_four(parts):
    a, b, c, d = parts
    return (
        (a + b[:, :128]).astype(BF16),
        (b[:, 128:] + c[:, :128]).astype(BF16),
        (c[:, 128:] + d).astype(BF16),
    )


def pack_kernel(order_ref, place_ref, q_ref, g_ref, k_ref, v_ref, out_ref, a_s, b_s):
    i = pl.program_id(0)
    at = pl.ds(pl.multiple_of(i // 2 * PD + HALF + i % 2 * PENCIL, PENCIL), PENCIL)
    a_s[at, :] = k_ref[...]
    b_s[at, :] = v_ref[...]

    @pl.when(i == PD // PENCIL - 1)
    def _():
        for half in range(2):
            rows = slice(half * HALF, (half + 1) * HALF)
            a_s[half * PD : half * PD + HALF, :] = q_ref[rows, :]
            b_s[half * PD : half * PD + HALF, :] = g_ref[rows, :]
        for turn in range(4):
            heads = range(turn, H, 4)
            offset = turn * HD % 128
            width = 128 if offset + HD <= 128 else 256
            parts = []
            for n, (_, cols, dst) in enumerate(WINDOWS):
                ref = (a_s, b_s)[n % 2]
                rows = slice(n // 2 * PD, (n // 2 + 1) * PD)
                x = [ref[rows, h * HD // 128 * 128 : h * HD // 128 * 128 + width] for h in heads]
                parts.append(mm(jnp.concatenate(x, axis=0), shift(width, cols, offset, dst)))
            for n, piece in enumerate(pack_four(parts)):
                for k, h in enumerate(heads):
                    out_ref[h, :, n * 128 : (n + 1) * 128] = piece[k * PD : (k + 1) * PD]


def pack(order, place, obj_query, grad_out, pattern_key, pattern_value):
    rows = pl.BlockSpec((PD, D), lambda i, order, place: (0, 0))
    block = pl.BlockSpec((PENCIL, D), lambda i, order, place: (order[place[0] + i] - place[1], 0))
    return pl.pallas_call(
        pack_kernel,
        out_shape=jax.ShapeDtypeStruct((H, PD, WIDE), BF16),
        grid_spec=pltpu.PrefetchScalarGridSpec(
            num_scalar_prefetch=2,
            grid=(PD // PENCIL,),
            in_specs=[rows, rows, block, block],
            out_specs=pl.BlockSpec((H, PD, WIDE), lambda i, order, place: (0, 0, 0)),
            scratch_shapes=[pltpu.VMEM((2 * PD, D), BF16)] * 2,
        ),
        compiler_params=pltpu.CompilerParams(vmem_limit_bytes=16 << 20),
        name="pack",
    )(away(order), place, *map(away, (obj_query, grad_out, pattern_key, pattern_value)))


def unpack(ref, stores, turned=False):
    half = ROWS // 2
    for n, (start, width, offset) in enumerate(WINDOWS):
        out, base = stores[n % 2]
        if out is None:
            continue
        at = slice(base + n // 2 * half, base + n // 2 * half + half)
        x = ref[:, :, start : start + width].reshape(half, width)
        if turned:
            out[:, at] = mm(turned_shift(width, offset), x, CONTRACT_LAST)[: out.shape[0]].astype(BF16)
        else:
            out[at, :] = mm(x, shift(width, 128, offset, 0)).astype(BF16)


def sweep(state, k_ref, v_ref, qt, gt):
    m, l, w = state
    rows, cols = k_ref.shape[0], qt.shape[1]
    s = mm(k_ref[...], qt).reshape(rows // SUB, SUB // 8, 8, cols)
    d = mm(v_ref[...], gt).reshape(rows // SUB, SUB // 8, 8, cols)
    for i in range(rows // SUB):
        top = jnp.maximum(m, jnp.max(s[i], axis=0))
        fade = jnp.exp2((m - top) * C2)
        e = jnp.exp2((s[i] - top[None]) * C2)
        m, l, w = top, l * fade + jnp.sum(e, axis=0), w * fade + jnp.sum(e * d[i], axis=0)
    return m, l, w


def write_stats(st_ref, n, state):
    m, l, w = state
    top = jnp.max(m, axis=0, keepdims=True)
    fade = jnp.exp2((m - top) * C2)
    row, cols = n // 2 * 4, slice(n % 2 * ROWS, (n % 2 + 1) * ROWS)
    st_ref[row : row + 1, cols] = top
    st_ref[row + 1 : row + 2, cols] = jnp.sum(l * fade, axis=0, keepdims=True)
    st_ref[row + 2 : row + 3, cols] = jnp.sum(w * fade, axis=0, keepdims=True)


def first_stats_kernel(qa_ref, qb_ref, kv_ref, st_ref, q_ref, g_ref, k_ref, v_ref):
    unpack(kv_ref, ((k_ref, 0), (v_ref, 0)))
    for n, ref in enumerate((qa_ref, qb_ref)):
        unpack(ref, ((q_ref, n * ROWS), (g_ref, n * ROWS)), turned=True)
    st_ref[...] = jnp.zeros_like(st_ref)
    for n in range(2):
        here = slice(n * ROWS, (n + 1) * ROWS)
        zero = jnp.zeros((8, ROWS), F32)
        state = (jnp.full((8, ROWS), NEG, F32), zero, zero)
        write_stats(st_ref, n, sweep(state, k_ref, v_ref, q_ref[:, here], g_ref[:, here]))


def first_stats(qa, qb, kv):
    return pl.pallas_call(
        first_stats_kernel,
        out_shape=[pltpu.VMEM((8, NQ // 2), F32)]
        + [pltpu.VMEM((128, 2 * ROWS), BF16)] * 2
        + [pltpu.VMEM((ROWS, 128), BF16)] * 2,
        in_specs=[VMEM] * 3,
        out_specs=[VMEM] * 5,
        cost_estimate=pl.CostEstimate(flops=NQ * NK * 256, transcendentals=NQ * NK // 4, bytes_accessed=2 << 20),
        compiler_params=pltpu.CompilerParams(vmem_limit_bytes=32 << 20),
        name="first_stats",
    )(*here(qa, qb, kv))


def stats_kernel(
    qa_ref, qb_ref, kv_ref, part_ref, q_own, g_own, k_own, v_own, st_ref, q_s, g_s, k_s, v_s
):
    unpack(kv_ref, ((k_s, 0), (v_s, 0)))
    for n, ref in enumerate((qa_ref, qb_ref)):
        unpack(ref, ((q_s, n * ROWS), (g_s, n * ROWS)), turned=True)
    st_ref[...] = jnp.zeros_like(st_ref)
    zero = jnp.zeros((8, ROWS), F32)
    for n in range(2):
        here = slice(n * ROWS, (n + 1) * ROWS)
        top, total, weighted = (part_ref[i : i + 1, here] for i in range(3))
        first = lax.broadcasted_iota(jnp.int32, (8, ROWS), 0) == 0
        state = (zero + top, jnp.where(first, total, zero), jnp.where(first, weighted, zero))
        write_stats(st_ref, n, sweep(state, k_s, v_s, q_own[:, here], g_own[:, here]))
    for n in range(2):
        here = slice(n * ROWS, (n + 1) * ROWS)
        qt, gt = q_s[:, here], g_s[:, here]
        state = sweep((jnp.full((8, ROWS), NEG, F32), zero, zero), k_own, v_own, qt, gt)
        write_stats(st_ref, 2 + n, sweep(state, k_s, v_s, qt, gt))


def stats(qa, qb, kv, first):
    return pl.pallas_call(
        stats_kernel,
        out_shape=pltpu.VMEM((8, NQ // 2), F32),
        in_specs=[VMEM] * 8,
        out_specs=VMEM,
        scratch_shapes=[pltpu.VMEM((128, 2 * ROWS), BF16)] * 2 + [pltpu.VMEM((ROWS, 128), BF16)] * 2,
        cost_estimate=pl.CostEstimate(flops=3 * NQ * NK * 256, transcendentals=NQ * NK, bytes_accessed=4 << 20),
        compiler_params=pltpu.CompilerParams(vmem_limit_bytes=36 << 20),
        name="stats",
    )(*here(qa, qb, kv, *first))


def rows_kernel(*refs):
    q_refs, kv_refs = refs[:N_Z], refs[N_Z : N_Z + 2]
    q_s, g_s, k_s, v_s, t_s = refs[N_Z + 2 :]
    for n, ref in enumerate(kv_refs):
        unpack(ref, ((k_s, n * ROWS), (v_s, n * ROWS)))
        unpack(ref, ((t_s, n * ROWS), (None, 0)), turned=True)
    for n, ref in enumerate(q_refs):
        unpack(ref, ((q_s, n * ROWS), (g_s, n * ROWS)))


def rows_of(queries, keys):
    return pl.pallas_call(
        rows_kernel,
        out_shape=[pltpu.VMEM((NQ, 128), BF16)] * 2
        + [pltpu.VMEM((NK, 128), BF16)] * 2
        + [pltpu.VMEM((HD, NK), BF16)],
        in_specs=[VMEM] * (N_Z + 2),
        out_specs=[VMEM] * 5,
        compiler_params=pltpu.CompilerParams(vmem_limit_bytes=24 << 20),
        name="rows_of",
    )(*here(*queries, *keys))


def block_of(ref, n):
    row, col = n // 2 * 4, n % 2 * ROWS
    return [ref[row + i : row + i + 1, col : col + ROWS] for i in range(3)]


def joined(parts):
    top = functools.reduce(jnp.maximum, [part[0] for part in parts])
    fades = [jnp.exp2((part[0] - top) * C2) for part in parts]
    total = sum(part[1] * fade for part, fade in zip(parts, fades))
    weighted = sum(part[2] * fade for part, fade in zip(parts, fades))
    return top * C2 + jnp.log2(total), weighted / total


def grads_kernel(key_block, blocks, takes_dq, takes_dkv, gives_dq, gives_dkv, *refs):
    refs = list(refs)
    q_s, g_s, k_s, v_s, t_s = refs[:5]
    st_refs, refs = refs[5 : 5 + N_Z], refs[5 + N_Z :]
    dq_in = refs.pop(0) if takes_dq else None
    dk_in, dv_in = (refs.pop(0), refs.pop(0)) if takes_dkv else (None, None)
    dq_outs = [refs.pop(0) for _ in (range(1) if gives_dq else blocks)]
    dkv_outs = [refs.pop(0) for _ in range(1 if gives_dkv else 2)]
    dq_s, dk_s, dv_s, log_s, mean_s = refs
    if gives_dq:
        dq_s = dq_outs[0]
    if not gives_dkv:
        dk_s, dv_s = dkv_outs
    for i, n in enumerate(blocks):
        log_now, mean_now = joined([block_of(st, n ^ t) for t, st in enumerate(st_refs)])
        here = slice(i * ROWS, (i + 1) * ROWS)
        log_s[:, here] = jnp.broadcast_to(log_now, (8, ROWS))
        mean_s[:, here] = jnp.broadcast_to(mean_now, (8, ROWS))
        dq_s[:, here] = dq_in[:, n * ROWS : (n + 1) * ROWS] if takes_dq else jnp.zeros((HD, ROWS), F32)

    def one_chunk(j, _):
        j0 = pl.multiple_of(j * TK, TK)
        k0 = pl.multiple_of(key_block * ROWS + j * TK, TK)
        kc = k_s[pl.ds(k0, TK), :]
        vc = v_s[pl.ds(k0, TK), :]
        kt = t_s[:, pl.ds(k0, TK)]
        if takes_dkv:
            dk, dv = dk_in[pl.ds(j0, TK), :], dv_in[pl.ds(j0, TK), :]
        else:
            dk = dv = jnp.zeros((TK, 128), F32)
        for i, n in enumerate(blocks):
            here = slice(i * ROWS, (i + 1) * ROWS)
            qt = q_s[n * ROWS : (n + 1) * ROWS, :]
            gt = g_s[n * ROWS : (n + 1) * ROWS, :]
            s = mm(kc, qt, CONTRACT_LAST).reshape(TK // 8, 8, ROWS)
            d = mm(vc, gt, CONTRACT_LAST).reshape(TK // 8, 8, ROWS)
            p = jnp.exp2(s * C2 - log_s[:, here][None])
            sg = ((d - mean_s[:, here][None]) * (p * SCALE)).astype(BF16).reshape(TK, ROWS)
            p = p.astype(BF16).reshape(TK, ROWS)
            dq_s[:, here] += mm(kt, sg)
            dk, dv = dk + mm(sg, qt), dv + mm(p, gt)
        dk_s[pl.ds(j0, TK), :] = dk.astype(dk_s.dtype)
        dv_s[pl.ds(j0, TK), :] = dv.astype(dv_s.dtype)
        return 0

    lax.fori_loop(0, ROWS // TK, one_chunk, 0, unroll=len(blocks) <= 2)
    place4 = [shift(HD, cols, 0, dst) for _, cols, dst in WINDOWS]
    half = ROWS // 2
    if gives_dkv:
        parts = [mm((dk_s, dv_s)[i % 2][i // 2 * half : (i // 2 + 1) * half, :HD], place4[i]) for i in range(4)]
        for k, piece in enumerate(pack_four(parts)):
            dkv_outs[0][:, :, k * 128 : (k + 1) * 128] = piece.reshape(N_G, HALF, 128)
    if not gives_dq:
        for i, ref in enumerate(dq_outs):
            parts = []
            for quarter in range(4):
                r0 = i * ROWS + quarter // 2 * half
                x = mm(dq_s[:, r0 : r0 + half].astype(BF16), place4[quarter], CONTRACT_FIRST)
                x = x.reshape(N_G, 2, PENCIL, x.shape[1])[:, quarter % 2]
                parts.append(x.reshape(N_G * PENCIL, x.shape[2]))
            for k, piece in enumerate(pack_four(parts)):
                ref[:, :, k * 128 : (k + 1) * 128] = piece.reshape(N_G, PENCIL, 128)


def grads(key_block, blocks, rows, statistics, dq=None, dkv=None, gives_dq=False, gives_dkv=True):
    taken = [*(() if dq is None else (dq,)), *(() if dkv is None else dkv)]
    size = len(blocks) * ROWS
    dq_out = [pltpu.VMEM((HD, size), F32)] if gives_dq else [pltpu.VMEM((N_G, PENCIL, WIDE), BF16)] * len(blocks)
    dkv_out = [pltpu.VMEM((N_G, HALF, WIDE), BF16)] if gives_dkv else [pltpu.VMEM((ROWS, 128), F32)] * 2
    return pl.pallas_call(
        functools.partial(grads_kernel, key_block, blocks, dq is not None, dkv is not None, gives_dq, gives_dkv),
        out_shape=dq_out + dkv_out,
        in_specs=[VMEM] * (5 + N_Z + len(taken)),
        out_specs=[VMEM] * len(dq_out + dkv_out),
        scratch_shapes=[pltpu.VMEM((8, 128) if gives_dq else (HD, size), F32)]
        + [pltpu.VMEM((ROWS, 128), BF16)] * 2
        + [pltpu.VMEM((8, size), F32)] * 2,
        cost_estimate=pl.CostEstimate(
            flops=10 * size * ROWS * 256, transcendentals=size * ROWS, bytes_accessed=1 << 20
        ),
        compiler_params=pltpu.CompilerParams(vmem_limit_bytes=40 << 20),
    )(*here(*rows, *statistics, *taken))


def meet_kernel(mine_ref, theirs_ref, send_ref):
    send_ref[...] = (mine_ref[...].astype(F32) + theirs_ref[...].astype(F32)).astype(BF16)


def meet(mine, theirs):
    return pl.pallas_call(
        meet_kernel,
        out_shape=pltpu.VMEM((N_G, PENCIL, WIDE), BF16),
        in_specs=[VMEM, VMEM],
        out_specs=VMEM,
        compiler_params=pltpu.CompilerParams(vmem_limit_bytes=16 << 20),
        name="meet",
    )(*here(mine, theirs))


def combine_kernel(*refs):
    out_ref = refs[-1]
    row = 0
    for parts in (refs[:2], refs[2:-1]):
        total = parts[0][...].astype(F32)
        for part in parts[1:]:
            total = total + part[...].astype(F32)
        out_ref[:, row : row + total.shape[1], :] = total.astype(BF16)
        row += total.shape[1]


def combine(parts):
    return pl.pallas_call(
        combine_kernel,
        out_shape=jax.ShapeDtypeStruct((N_G, HALF + PENCIL, WIDE), BF16),
        in_specs=[VMEM] * len(parts),
        out_specs=VMEM,
        compiler_params=pltpu.CompilerParams(vmem_limit_bytes=16 << 20),
        name="combine",
    )(*here(*parts))


def finish_kernel(got_ref, query_ref, key_ref, value_ref):
    for h in range(H):
        here = slice(h * HD, (h + 1) * HD)
        for half in range(2):
            lane = half * 2 * HD
            rows = slice(half * HALF, (half + 1) * HALF)
            key_ref[rows, here] = got_ref[h, :HALF, lane : lane + HD]
            value_ref[rows, here] = got_ref[h, :HALF, lane + HD : lane + 2 * HD]
        for quarter in range(4):
            rows = slice(quarter * PENCIL, (quarter + 1) * PENCIL)
            query_ref[rows, here] = got_ref[h, HALF:, quarter * HD : (quarter + 1) * HD]


def finish(got):
    return pl.pallas_call(
        finish_kernel,
        out_shape=[jax.ShapeDtypeStruct((PD, D), BF16)] * 3,
        in_specs=[VMEM],
        out_specs=[VMEM] * 3,
        compiler_params=pltpu.CompilerParams(vmem_limit_bytes=16 << 20),
        name="finish",
    )(got)


def over_a(x):
    return lax.ppermute(x, Z, ((0, 3), (3, 0), (1, 2), (2, 1)))


def over_b(x):
    return lax.ppermute(x, Z, ((0, 1), (1, 0), (2, 3), (3, 2)))


def over_core(x):
    return lax.ppermute(x, CORE, ((0, 1), (1, 0)))


def to_heads(x):
    return lax.all_to_all(x, HEADS, 0, 0, tiled=True)


def layer(obj_query, grad_out, pattern_key, pattern_value, pencil_order):
    place = jnp.stack(
        [lax.axis_index(BLK_GRP) * (PD // PENCIL), lax.axis_index(GRP) * (pattern_key.shape[0] // PENCIL)]
    ).astype(jnp.int32)
    sent = pack(pencil_order, place, obj_query, grad_out, pattern_key, pattern_value)
    got = to_heads(sent)
    queries, keys = [got[:, :HALF]], [got[:, HALF:]]
    queries.append(over_core(queries[0]))
    queries.append(over_b(queries[0]))
    keys.append(over_a(keys[0]))
    first = first_stats(queries[0], queries[1], keys[0])
    queries.append(over_core(queries[2]))
    statistics = [stats(queries[2], queries[3], keys[1], first)]
    third = over_b(statistics[0])
    statistics += [over_core(statistics[0]), third, over_core(third)]
    rows = rows_of(queries, keys)
    dq, keys_there = grads(1, (0, 1, 2, 3), rows, statistics, gives_dq=True)
    keys_got = over_a(keys_there)
    beside, both, *dkv = grads(0, (2, 3), rows, statistics, dq, gives_dkv=False)
    both_got = over_core(both)
    send = meet(beside, both_got)
    beside_got = over_b(send)
    own, core, keys_here = grads(0, (0, 1), rows, statistics, dq, dkv)
    core_got = over_core(core)
    total = combine([keys_here, keys_got, own, core_got, beside_got])
    total = to_heads(total)
    return tuple(finish(total))


def solution(mesh):
    split = Mesh(mesh.devices.reshape(4, 2, 2, 4, 2), BLK_GRP)
    return jax.shard_map(
        layer,
        mesh=split,
        in_specs=(P(BLK_GRP, None), P(BLK_GRP, None), P(GRP, None), P(GRP, None), P()),
        out_specs=(P(BLK_GRP, None), P(BLK_GRP, None), P(BLK_GRP, None)),
        check_vma=False,
    )
```
